32 devices in a mesh: pix: 8 (over y, x, core), tm: 4 (over z).
Axes of the slice: x: 2, y: 2, z: 4, core: 2. Of those that a mesh axis runs over, the one named last changes fastest.
Arguments:
- fields: float32 [256, 8, 2, 1024], P('pix', None, None, 'tm'), may hold values from -6 to 6
- profiles: bfloat16 [16384, 256], P('pix'), may hold values from -0.5 to 0.5
- phase: float32 [256, 1024], P(('pix', 'tm')), may hold values from -3.140625 to 3.140625
Outputs:
- advanced: float32 [256, 8, 2, 1024], P('pix', None, None, 'tm')
The draws below stay inside these ranges and needn't reach their ends.
All inputs are finite; a program needn't handle non-finite values.
Results may differ from the reference program's by a relative error of at most 0.003.
Values may be sent and summed in bfloat16 or wider, within the bound.
No kernel may reach another device: no remote copies, remote signals or barrier semaphores. Data moves between devices by JAX's collectives and lax.ppermute only.
A program may use at most 64 MiB of HBM per device.

```python
import math
import jax
import jax.numpy as jnp
from jax import lax

MODES = 256
TIMES = 1024
PIX_DEV = 2048
BATCH = 8
PIXELS = 16384


def raised(array, own_key, source, target, parts, factor):
    owner, partner = [(jnp.arange(array.shape[position]) // (array.shape[position] // parts)).reshape([-1 if axis == position else 1 for axis in range(array.ndim)]) for position in (source, target)]
    chosen = jax.random.permutation(own_key, parts)[partner]
    strong = (owner == chosen) | (owner == (partner + parts // 2) % parts)
    return jnp.where(strong, factor * array, array)


def steps_of(own_key, shape, cuts, least, largest):
    factor_of = 1.0
    for axis_at, parts in cuts:
        steps = jax.random.uniform(jax.random.fold_in(jax.random.fold_in(own_key, 6), axis_at), (parts,), jnp.float32, least / len(cuts), largest / len(cuts))
        factor_of = factor_of * jnp.repeat(jnp.exp(steps), shape[axis_at] // parts).reshape((-1,) + (1,) * (len(shape) - 1 - axis_at))
    return factor_of


def normal_values(rng, dims, spread, most, cuts=(), held_as=jnp.bfloat16):
    loudness = steps_of(rng, dims, cuts, -0.22, 0.18) if cuts else 1.0
    array = jax.random.normal(rng, dims, jnp.float32) * spread * loudness
    return jnp.minimum(jnp.maximum(array, -most), most).astype(held_as)


def noise_with(own_key, extent, deviation, bound, split, heavy, kind=jnp.bfloat16):
    entries = deviation * jax.random.normal(own_key, extent, jnp.float32)
    if split:
        entries = entries * steps_of(own_key, extent, split, -0.22, 0.18)
    return jnp.clip(raised(entries, jax.random.fold_in(own_key, 3), *heavy), -bound, bound).astype(kind)


def setup_inputs(seed: int = 0) -> dict:
    streams_of = jax.random.split(jax.random.key(seed), 4)
    return {
        "fields": normal_values(streams_of[0], (MODES, BATCH, 2, TIMES), 1.0, 6.0, ((0, 8), (3, 4)), jnp.float32),
        "profiles": noise_with(streams_of[1], (PIXELS, MODES), MODES ** -0.5, 0.5, ((0, 8),), (0, 1, 8, 2.0)),
        "phase": jnp.clip(jax.random.uniform(streams_of[2], (MODES, TIMES), jnp.float32, -3.140625, 3.140625), -3.140625, 3.140625),
    }


def reference(fields, profiles, phase):
    count = profiles.shape[0]
    modes = fields.shape[0]
    block = PIX_DEV
    flat = fields.astype(jnp.bfloat16).reshape(modes, -1)

    def visit(total, start):
        rows = lax.dynamic_slice_in_dim(profiles, start, block, 0)
        spatial = jnp.dot(rows, flat, preferred_element_type=jnp.float32).reshape(block, BATCH, 2, TIMES)
        real_part = spatial[:, :, 0]
        imag_part = spatial[:, :, 1]
        power = real_part * real_part + imag_part * imag_part
        nonlin = jnp.stack([power * real_part, power * imag_part], axis=2).astype(jnp.bfloat16).reshape(block, -1)
        total = total + lax.dot_general(rows, nonlin, (((0,), (0,)), ((), ())), preferred_element_type=jnp.float32)
        return (total, None)
    starts = jnp.arange(count // block, dtype=jnp.int32) * block
    kerr, unused = lax.scan(visit, jnp.zeros((modes, BATCH * 2 * TIMES), jnp.float32), starts)
    kerr = kerr.reshape(modes, BATCH, 2, TIMES) * (1.0 / math.sqrt(count))
    stepped_re = fields[:, :, 0] - kerr[:, :, 1]
    stepped_im = fields[:, :, 1] + kerr[:, :, 0]
    spectrum = jnp.fft.fft(stepped_re + 1j * stepped_im, axis=-1)
    rotated = spectrum * jnp.exp(1j * phase)[:, None, :]
    result = jnp.fft.ifft(rotated, axis=-1)
    return jnp.stack([jnp.real(result), jnp.imag(result)], axis=2).astype(jnp.float32)
```

```python
import functools
import math

import jax
import jax.numpy as jnp
import numpy as np
from jax import lax
from jax.experimental import pallas as pl
from jax.experimental.pallas import tpu as pltpu
from jax.sharding import PartitionSpec as P

BF16 = jnp.bfloat16
F32 = jnp.float32
CHUNKS = (1,)
VMEM = pl.BlockSpec(memory_space=pltpu.VMEM)


def call(kernel, name, outs, scratch=(), cost=None):
    def run(*args):
        return pl.pallas_call(
            kernel,
            out_shape=tuple(jax.ShapeDtypeStruct(*out) for out in outs),
            in_specs=[VMEM] * len(args),
            out_specs=tuple(VMEM for _ in outs),
            scratch_shapes=[pltpu.VMEM(*item) for item in scratch],
            compiler_params=pltpu.CompilerParams(vmem_limit_bytes=56 * 2**20),
            cost_estimate=None
            if cost is None
            else pl.CostEstimate(flops=cost[0], bytes_accessed=cost[1], transcendentals=0),
            name=name,
        )(*args)

    return run


def swap_pix(value, mask, size):
    return lax.ppermute(value, "pix", [(i, i ^ mask) for i in range(size)])


def swap_tm(value, mask, size):
    return lax.ppermute(value, "tm", [(i, i ^ mask) for i in range(size)])


def split_kernel(starts, sizes, fields, *outs):
    half = fields.shape[1] // 2
    core = lax.axis_index("pix") % 2
    for n, (start, nb) in enumerate(zip(starts, sizes)):
        own, other = outs[2 * n], outs[2 * n + 1]
        for c in range(2):
            for b in range(nb):
                own[c * nb + b] = fields[:, core * half + start + b, c, :]
                other[c * nb + b] = fields[:, (1 - core) * half + start + b, c, :]


def modal_kernel(own, other, full, modal):
    rows = own.shape[1]
    core = lax.axis_index("pix") % 2
    mine = pl.multiple_of(core * rows, rows)
    theirs = pl.multiple_of((1 - core) * rows, rows)
    for k in range(own.shape[0]):
        value = own[k]
        full[k, pl.ds(mine, rows), :] = value
        modal[k, pl.ds(mine, rows), :] = value.astype(BF16)
        value = other[k]
        full[k, pl.ds(theirs, rows), :] = value
        modal[k, pl.ds(theirs, rows), :] = value.astype(BF16)


def turn_kernel(rows, chips, profiles, turned):
    chip = lax.axis_index("pix") // 2
    step = 256
    for i in range(profiles.shape[0] // step):
        block = profiles[i * step : (i + 1) * step, :].T
        for j in range(chips):
            place = pl.multiple_of((chip ^ j) * rows, rows)
            turned[pl.ds(place, rows), i * step : (i + 1) * step] = block[j * rows : (j + 1) * rows]


def kerr_kernel(nb, chips, tile, *refs):
    profiles, turned = refs[0:2], refs[2:4]
    blocks = refs[4 : 4 + chips]
    outs = refs[4 + chips : 4 + 2 * chips]
    gathered, cubed = refs[4 + 2 * chips :]
    chip = lax.axis_index("pix") // 2
    rows, time = blocks[0].shape[1:]
    pixels = profiles[0].shape[0]

    def one(b, carry):
        for j in range(chips):
            place = pl.multiple_of((chip ^ j) * rows, rows)
            for c in range(2):
                gathered[pl.ds(place, rows), c * time : (c + 1) * time] = blocks[j][c * nb + b]
        modal = gathered[...]
        for h in range(2):
            for i in range(pixels // tile):
                spatial = jnp.dot(
                    profiles[h][i * tile : (i + 1) * tile, :], modal, preferred_element_type=F32
                )
                real, imag = spatial[:, :time], spatial[:, time:]
                power = real * real + imag * imag
                at = h * pixels + i * tile
                cubed[at : at + tile, :time] = (power * real).astype(BF16)
                cubed[at : at + tile, time:] = (power * imag).astype(BF16)
        kerr = jnp.dot(turned[0][...], cubed[:pixels], preferred_element_type=F32) + jnp.dot(
            turned[1][...], cubed[pixels:], preferred_element_type=F32
        )
        for j in range(chips):
            for c in range(2):
                outs[j][c * nb + b] = kerr[
                    j * rows : (j + 1) * rows, c * time : (c + 1) * time
                ].astype(outs[j].dtype)
        return carry

    lax.fori_loop(0, nb, one, 0)


def step_kernel(nb, scale, times, full, *refs):
    chips = len(refs) - times - 1
    parts, outs, stepped = refs[:chips], refs[chips:-1], refs[-1]
    z = lax.axis_index("tm")
    rows = full.shape[1]
    cut = rows // 2 // times

    def total(k):
        value = parts[0][k]
        for part in parts[1:]:
            value = value + part[k].astype(F32)
        return value * scale

    for b in range(nb):
        stepped[b] = full[b] - total(nb + b)
        stepped[nb + b] = full[nb + b] + total(b)
    for j in range(times):
        for h in range(2):
            at = pl.multiple_of(h * (rows // 2) + (z ^ j) * cut, cut)
            for k in range(2 * nb):
                outs[j][k, h * cut : (h + 1) * cut, :] = stepped[k, pl.ds(at, cut), :].astype(
                    outs[j].dtype
                )


def product(value, high, low):
    top = value.astype(BF16)
    rest = (value - top.astype(F32)).astype(BF16)
    out = jnp.dot(top, high, preferred_element_type=F32)
    out = out + jnp.dot(rest, high, preferred_element_type=F32)
    return out + jnp.dot(top, low, preferred_element_type=F32)


def weighted(terms, powers):
    real, imag = None, None
    for (re, im), power in zip(terms, powers):
        re, im = ((re, im), (-im, re), (-re, -im), (im, -re))[power % 4]
        real = re if real is None else real + re
        imag = im if imag is None else imag + im
    return real, imag


def wave_kernel(nb, times, *refs):
    blocks = refs[:times]
    phase_cos, phase_sin, cos_high, cos_low, sin_high, sin_low, twist_cos, twist_sin = refs[
        times : times + 8
    ]
    outs = refs[times + 8 : 2 * times + 8]
    held, back = refs[2 * times + 8 :]
    z = lax.axis_index("tm")
    rows, time = blocks[0].shape[1:]
    size = nb * rows
    length = times * time
    for j in range(times):
        held[z ^ j] = blocks[j][...].astype(F32)
    here = [
        (held[a, :nb].reshape(size, time), held[a, nb:].reshape(size, time)) for a in range(times)
    ]
    real, imag = [], []
    for s in range(times):
        re, im = weighted(here, [-a * s for a in range(times)])
        tc, ts = twist_cos[s : s + 1, :], twist_sin[s : s + 1, :]
        real.append(re * tc + im * ts)
        imag.append(im * tc - re * ts)
    real, imag = jnp.concatenate(real, axis=0), jnp.concatenate(imag, axis=0)
    ch, cl, sh, sl = cos_high[...], cos_low[...], sin_high[...], sin_low[...]
    freq_re = product(real, ch, cl) + product(imag, sh, sl)
    freq_im = product(imag, ch, cl) - product(real, sh, sl)
    shape = (times, nb, rows, time)
    pc = jnp.broadcast_to(phase_cos[...][:, None], shape).reshape(times * size, time)
    ps = jnp.broadcast_to(phase_sin[...][:, None], shape).reshape(times * size, time)
    spun_re = freq_re * pc - freq_im * ps
    spun_im = freq_re * ps + freq_im * pc
    back_re = product(spun_re, ch, cl) - product(spun_im, sh, sl)
    back_im = product(spun_im, ch, cl) + product(spun_re, sh, sl)
    terms = []
    for s in range(times):
        tc, ts = twist_cos[s : s + 1, :] / length, twist_sin[s : s + 1, :] / length
        re, im = back_re[s * size : (s + 1) * size], back_im[s * size : (s + 1) * size]
        terms.append((re * tc - im * ts, im * tc + re * ts))
    for a in range(times):
        re, im = weighted(terms, [a * s for s in range(times)])
        back[a, :nb] = re.reshape(nb, rows, time)
        back[a, nb:] = im.reshape(nb, rows, time)
    for j in range(times):
        outs[j][...] = back[z ^ j].astype(outs[j].dtype)


def part_kernel(times, *refs):
    blocks, (own, other), (held,) = refs[:times], refs[times : times + 2], refs[times + 2 :]
    core = lax.axis_index("pix") % 2
    z = lax.axis_index("tm")
    cut = blocks[0].shape[1] // 2
    for j in range(times):
        held[...] = blocks[j][...].astype(F32)
        at = pl.multiple_of((z ^ j) * cut, cut)
        mine = pl.multiple_of(core * cut, cut)
        theirs = pl.multiple_of((1 - core) * cut, cut)
        own[:, pl.ds(at, cut), :] = held[:, pl.ds(mine, cut), :]
        other[:, pl.ds(at, cut), :] = held[:, pl.ds(theirs, cut), :]


def join_kernel(starts, sizes, *refs):
    out = refs[-1]
    half = out.shape[1] // 2
    core = lax.axis_index("pix") % 2
    for n, (start, nb) in enumerate(zip(starts, sizes)):
        own, other = refs[2 * n], refs[2 * n + 1]
        for c in range(2):
            for b in range(nb):
                out[:, core * half + start + b, c, :] = own[c * nb + b]
                out[:, (1 - core) * half + start + b, c, :] = other[c * nb + b].astype(F32)


def tables(times, time):
    index = np.arange(time)
    angle = 2.0 * np.pi / time * (index[:, None] * index[None, :] % time)
    length = times * time
    twist = 2.0 * np.pi / length * (np.arange(times)[:, None] * index[None, :] % length)
    out = []
    for table in (np.cos(angle), np.sin(angle)):
        high = table.astype(np.float32).astype(jnp.bfloat16)
        low = (table - high.astype(np.float64)).astype(np.float32).astype(jnp.bfloat16)
        out += [jnp.asarray(high), jnp.asarray(low)]
    return out + [jnp.asarray(f(twist).astype(np.float32)) for f in (np.cos, np.sin)]


def fast_body(pix, times, fields, profiles, phase):
    modes, batch, _, time = fields.shape
    chips, half = pix // 2, batch // 2
    pixels = profiles.shape[0]
    rows = 2 * modes
    cut = rows // times
    scale = 1.0 / math.sqrt(pixels * pix)
    sizes = [half * part // sum(CHUNKS) for part in CHUNKS]
    starts = [sum(sizes[:n]) for n in range(len(sizes))]
    core = lax.axis_index("pix") % 2

    halves = call(
        functools.partial(split_kernel, starts, sizes),
        "split",
        [((2 * nb, modes, time), F32) for nb in sizes for _ in range(2)],
    )(fields)
    others = [swap_pix(halves[2 * n + 1], 1, pix) for n in range(len(sizes))]
    profiles_other = swap_pix(profiles, 1, pix)
    phase_other = swap_pix(phase, 1, pix)

    fulls, gathers = [], []
    for n, nb in enumerate(sizes):
        full, modal = call(
            modal_kernel, "modal", [((2 * nb, rows, time), F32), ((2 * nb, rows, time), BF16)]
        )(halves[2 * n], others[n])
        fulls.append(full)
        gathers.append([modal] + [swap_pix(modal, 2 * j, pix) for j in range(1, chips)])

    turn = call(
        functools.partial(turn_kernel, rows, chips), "turn", [((chips * rows, pixels), BF16)]
    )
    turned = turn(profiles)[0], turn(profiles_other)[0]

    low = jnp.where(core == 0, phase, phase_other)
    high = jnp.where(core == 0, phase_other, phase)
    angles = jnp.concatenate([low, high], axis=0).reshape(cut, time, times).transpose(2, 0, 1)
    phase_cos, phase_sin = jnp.cos(angles), jnp.sin(angles)
    consts = tables(times, time)

    finals = []
    for n, nb in enumerate(sizes):
        block = (2 * nb, rows, time)
        parts = call(
            functools.partial(kerr_kernel, nb, chips, 512),
            "kerr",
            [(block, F32)] + [(block, BF16)] * (chips - 1),
            [((chips * rows, 2 * time), BF16), ((2 * pixels, 2 * time), BF16)],
        )(profiles, profiles_other, *turned, *gathers[n])
        sums = [parts[0]] + [swap_pix(parts[j], 2 * j, pix) for j in range(1, chips)]
        block = (2 * nb, cut, time)
        pieces = call(
            functools.partial(step_kernel, nb, scale, times),
            "step",
            [(block, F32)] + [(block, BF16)] * (times - 1),
            [((2 * nb, rows, time), F32)],
        )(fulls[n], *sums)
        pieces = [pieces[0]] + [swap_tm(pieces[j], j, times) for j in range(1, times)]
        pieces = call(
            functools.partial(wave_kernel, nb, times),
            "wave",
            [(block, F32)] + [(block, BF16)] * (times - 1),
            [((times,) + block, F32)] * 2,
        )(*pieces, phase_cos, phase_sin, *consts)
        pieces = [pieces[0]] + [swap_tm(pieces[j], j, times) for j in range(1, times)]
        own, other = call(
            functools.partial(part_kernel, times),
            "part",
            [((2 * nb, modes, time), F32), ((2 * nb, modes, time), F32)],
            [(block, F32)],
        )(*pieces)
        finals += [own, swap_pix(other, 1, pix)]
    return call(functools.partial(join_kernel, starts, sizes), "join", [(fields.shape, F32)])(
        *finals
    )[0]


def split_length(length):
    first = 2 ** ((length.bit_length() - 1) // 2)
    return (first, length // first)


def small_table(size):
    index = jnp.arange(size, dtype=jnp.int32)
    product = index[:, None] * index[None, :] % size
    angles = product.astype(jnp.float32) * (2.0 * math.pi / size)
    return (jnp.cos(angles), jnp.sin(angles))


def twiddles(first, second, length):
    rows = jnp.arange(first, dtype=jnp.int32)
    cols = jnp.arange(second, dtype=jnp.int32)
    product = rows[:, None] * cols[None, :] % length
    angles = product.astype(jnp.float32) * (2.0 * math.pi / length)
    return (jnp.cos(angles), jnp.sin(angles))


def contract_last(values, table):
    return jnp.einsum(
        "mbkv,vq->mbkq",
        values,
        table,
        precision=lax.Precision.HIGHEST,
        preferred_element_type=jnp.float32,
    )


def contract_third(values, table):
    return jnp.einsum(
        "mbuv,uk->mbkv",
        values,
        table,
        precision=lax.Precision.HIGHEST,
        preferred_element_type=jnp.float32,
    )


def dispersed(values, phase_rows, length):
    first, second = split_length(length)
    cos_first, sin_first = small_table(first)
    cos_second, sin_second = small_table(second)
    twist_cos, twist_sin = twiddles(first, second, length)
    modes_here = values.shape[0]
    batch = values.shape[1]
    real_part = values[:, :, 0].reshape(modes_here, batch, first, second)
    imag_part = values[:, :, 1].reshape(modes_here, batch, first, second)
    section_re = contract_third(real_part, cos_first) + contract_third(imag_part, sin_first)
    section_im = contract_third(imag_part, cos_first) - contract_third(real_part, sin_first)
    turned_re = section_re * twist_cos + section_im * twist_sin
    turned_im = section_im * twist_cos - section_re * twist_sin
    freq_re = contract_last(turned_re, cos_second) + contract_last(turned_im, sin_second)
    freq_im = contract_last(turned_im, cos_second) - contract_last(turned_re, sin_second)
    ordered = jnp.transpose(phase_rows.reshape(modes_here, second, first), (0, 2, 1))[:, None]
    phase_cos = jnp.cos(ordered)
    phase_sin = jnp.sin(ordered)
    spun_re = freq_re * phase_cos - freq_im * phase_sin
    spun_im = freq_re * phase_sin + freq_im * phase_cos
    back_re = contract_last(spun_re, cos_second) - contract_last(spun_im, sin_second)
    back_im = contract_last(spun_im, cos_second) + contract_last(spun_re, sin_second)
    again_re = back_re * twist_cos - back_im * twist_sin
    again_im = back_im * twist_cos + back_re * twist_sin
    out_re = contract_third(again_re, cos_first) - contract_third(again_im, sin_first)
    out_im = contract_third(again_im, cos_first) + contract_third(again_re, sin_first)
    out_re = out_re.reshape(modes_here, batch, length) / length
    out_im = out_im.reshape(modes_here, batch, length) / length
    return jnp.stack([out_re, out_im], axis=2)


def body(fields, profiles, phase):
    mode_local = fields.shape[0]
    batch = fields.shape[1]
    time_local = fields.shape[3]
    pixel_local = profiles.shape[0]
    length = time_local * lax.axis_size("tm")
    scale = 1.0 / math.sqrt(pixel_local * lax.axis_size("pix"))
    modal = fields.astype(jnp.bfloat16)
    piece = lax.all_gather(modal, "pix", axis=0, tiled=True)
    columns = profiles
    spatial = jnp.dot(
        columns, piece.reshape(piece.shape[0], -1), preferred_element_type=jnp.float32
    )
    spatial = spatial.reshape(pixel_local, batch, 2, time_local)
    real_part = spatial[:, :, 0]
    imag_part = spatial[:, :, 1]
    power = real_part * real_part + imag_part * imag_part
    nonlin = (
        jnp.stack([power * real_part, power * imag_part], axis=2)
        .astype(jnp.bfloat16)
        .reshape(pixel_local, -1)
    )
    columns = profiles
    kerr = lax.psum_scatter(
        lax.dot_general(
            columns, nonlin, (((0,), (0,)), ((), ())), preferred_element_type=jnp.float32
        ),
        "pix",
        scatter_dimension=0,
        tiled=True,
    )
    kerr = kerr.reshape(mode_local, batch, 2, time_local) * scale
    stepped = jnp.stack([fields[:, :, 0] - kerr[:, :, 1], fields[:, :, 1] + kerr[:, :, 0]], axis=2)
    result = dispersed(
        lax.all_to_all(stepped, "tm", split_axis=0, concat_axis=3, tiled=True), phase, length
    )
    return lax.all_to_all(result, "tm", split_axis=3, concat_axis=0, tiled=True)


def solution(mesh):
    pix, times = mesh.shape["pix"], mesh.shape["tm"]

    def run(fields, profiles, phase):
        modes, batch, _, time = fields.shape
        fits = (
            pix % 2 == 0
            and pix & (pix - 1) == 0
            and times == 4
            and modes % (8 * times) == 0
            and batch % 2 == 0
            and time % 256 == 0
            and profiles.shape[0] % 512 == 0
        )
        if fits:
            return fast_body(pix, times, fields, profiles, phase)
        return body(fields, profiles, phase)

    return jax.shard_map(
        run,
        mesh=mesh,
        in_specs=(P("pix", None, None, "tm"), P("pix", None), P(("pix", "tm"), None)),
        out_specs=P("pix", None, None, "tm"),
        check_vma=False,
    )
```

```python
import functools
import math

import jax
import jax.numpy as jnp
import numpy as np
from jax import lax
from jax.experimental import pallas as pl
from jax.experimental.pallas import tpu as pltpu
from jax.sharding import PartitionSpec as P

BF16 = jnp.bfloat16
F32 = jnp.float32
CHUNKS = (1,)
VMEM = pl.BlockSpec(memory_space=pltpu.VMEM)


def size_of(shape, dtype):
    return math.prod(shape) * jnp.dtype(dtype).itemsize


def call(kernel, name, outs, scratch=(), flops=0):
    def run(*args):
        moved = sum(size_of(item.shape, item.dtype) for item in args)
        moved += sum(size_of(*out) for out in outs)
        held = sum(size_of(*item) for item in scratch)
        return pl.pallas_call(
            kernel,
            out_shape=tuple(jax.ShapeDtypeStruct(*out) for out in outs),
            in_specs=[VMEM] * len(args),
            out_specs=tuple(VMEM for _ in outs),
            scratch_shapes=[pltpu.VMEM(*item) for item in scratch],
            compiler_params=pltpu.CompilerParams(vmem_limit_bytes=moved + held + 3 * 2**20),
            cost_estimate=pl.CostEstimate(flops=flops, bytes_accessed=moved, transcendentals=0),
            name=name,
        )(*args)

    return run


def swap_pix(value, mask, size):
    return lax.ppermute(value, "pix", [(i, i ^ mask) for i in range(size)])


def swap_tm(value, mask, size):
    return lax.ppermute(value, "tm", [(i, i ^ mask) for i in range(size)])


def split_kernel(starts, sizes, fields, *outs):
    half = fields.shape[1] // 2
    core = lax.axis_index("pix") % 2
    for n, (start, nb) in enumerate(zip(starts, sizes)):
        own, other = outs[2 * n], outs[2 * n + 1]
        for c in range(2):
            for b in range(nb):
                own[c * nb + b] = fields[:, core * half + start + b, c, :]
                other[c * nb + b] = fields[:, (1 - core) * half + start + b, c, :]


def modal_kernel(own, other, full, modal):
    rows = own.shape[1]
    core = lax.axis_index("pix") % 2
    mine = pl.multiple_of(core * rows, rows)
    theirs = pl.multiple_of((1 - core) * rows, rows)
    for k in range(own.shape[0]):
        value = own[k]
        full[k, pl.ds(mine, rows), :] = value
        modal[k, pl.ds(mine, rows), :] = value.astype(BF16)
        value = other[k]
        full[k, pl.ds(theirs, rows), :] = value
        modal[k, pl.ds(theirs, rows), :] = value.astype(BF16)


def turn_kernel(rows, chips, profiles, turned):
    chip = lax.axis_index("pix") // 2
    step = 256
    for i in range(profiles.shape[0] // step):
        block = profiles[i * step : (i + 1) * step, :].T
        for j in range(chips):
            place = pl.multiple_of((chip ^ j) * rows, rows)
            turned[pl.ds(place, rows), i * step : (i + 1) * step] = block[j * rows : (j + 1) * rows]


def kerr_kernel(nb, chips, tile, *refs):
    profiles, turned = refs[0:2], refs[2:4]
    blocks = refs[4 : 4 + chips]
    outs = refs[4 + chips : 4 + 2 * chips]
    gathered, cubed = refs[4 + 2 * chips :]
    chip = lax.axis_index("pix") // 2
    rows, time = blocks[0].shape[1:]
    pixels = profiles[0].shape[0]

    def one(b, carry):
        for j in range(chips):
            place = pl.multiple_of((chip ^ j) * rows, rows)
            for c in range(2):
                gathered[pl.ds(place, rows), c * time : (c + 1) * time] = blocks[j][c * nb + b]
        modal = gathered[...]
        for h in range(2):
            for i in range(pixels // tile):
                spatial = jnp.dot(
                    profiles[h][i * tile : (i + 1) * tile, :], modal, preferred_element_type=F32
                )
                real, imag = spatial[:, :time], spatial[:, time:]
                power = real * real + imag * imag
                at = h * pixels + i * tile
                cubed[at : at + tile, :time] = (power * real).astype(BF16)
                cubed[at : at + tile, time:] = (power * imag).astype(BF16)
        kerr = jnp.dot(turned[0][...], cubed[:pixels], preferred_element_type=F32) + jnp.dot(
            turned[1][...], cubed[pixels:], preferred_element_type=F32
        )
        for j in range(chips):
            for c in range(2):
                outs[j][c * nb + b] = kerr[
                    j * rows : (j + 1) * rows, c * time : (c + 1) * time
                ].astype(outs[j].dtype)
        return carry

    lax.fori_loop(0, nb, one, 0)


def step_kernel(nb, scale, times, full, *refs):
    chips = len(refs) - times - 1
    parts, outs, stepped = refs[:chips], refs[chips:-1], refs[-1]
    z = lax.axis_index("tm")
    rows = full.shape[1]
    cut = rows // 2 // times

    def total(k):
        value = parts[0][k]
        for part in parts[1:]:
            value = value + part[k].astype(F32)
        return value * scale

    for b in range(nb):
        stepped[b] = full[b] - total(nb + b)
        stepped[nb + b] = full[nb + b] + total(b)
    for j in range(times):
        for h in range(2):
            at = pl.multiple_of(h * (rows // 2) + (z ^ j) * cut, cut)
            for k in range(2 * nb):
                outs[j][k, h * cut : (h + 1) * cut, :] = stepped[k, pl.ds(at, cut), :].astype(
                    outs[j].dtype
                )


def product(value, high, low):
    top = value.astype(BF16)
    rest = (value - top.astype(F32)).astype(BF16)
    out = jnp.dot(top, high, preferred_element_type=F32)
    out = out + jnp.dot(rest, high, preferred_element_type=F32)
    return out + jnp.dot(top, low, preferred_element_type=F32)


def weighted(terms, powers):
    real, imag = None, None
    for (re, im), power in zip(terms, powers):
        re, im = ((re, im), (-im, re), (-re, -im), (im, -re))[power % 4]
        real = re if real is None else real + re
        imag = im if imag is None else imag + im
    return real, imag


def wave_kernel(nb, times, *refs):
    blocks = refs[:times]
    phase_cos, phase_sin, cos_high, cos_low, sin_high, sin_low, twist_cos, twist_sin = refs[
        times : times + 8
    ]
    outs = refs[times + 8 : 2 * times + 8]
    held, back = refs[2 * times + 8 :]
    z = lax.axis_index("tm")
    rows, time = blocks[0].shape[1:]
    size = nb * rows
    length = times * time
    for j in range(times):
        held[z ^ j] = blocks[j][...].astype(F32)
    here = [
        (held[a, :nb].reshape(size, time), held[a, nb:].reshape(size, time)) for a in range(times)
    ]
    real, imag = [], []
    for s in range(times):
        re, im = weighted(here, [-a * s for a in range(times)])
        tc, ts = twist_cos[s : s + 1, :], twist_sin[s : s + 1, :]
        real.append(re * tc + im * ts)
        imag.append(im * tc - re * ts)
    real, imag = jnp.concatenate(real, axis=0), jnp.concatenate(imag, axis=0)
    ch, cl, sh, sl = cos_high[...], cos_low[...], sin_high[...], sin_low[...]
    freq_re = product(real, ch, cl) + product(imag, sh, sl)
    freq_im = product(imag, ch, cl) - product(real, sh, sl)
    shape = (times, nb, rows, time)
    pc = jnp.broadcast_to(phase_cos[...][:, None], shape).reshape(times * size, time)
    ps = jnp.broadcast_to(phase_sin[...][:, None], shape).reshape(times * size, time)
    spun_re = freq_re * pc - freq_im * ps
    spun_im = freq_re * ps + freq_im * pc
    back_re = product(spun_re, ch, cl) - product(spun_im, sh, sl)
    back_im = product(spun_im, ch, cl) + product(spun_re, sh, sl)
    terms = []
    for s in range(times):
        tc, ts = twist_cos[s : s + 1, :] / length, twist_sin[s : s + 1, :] / length
        re, im = back_re[s * size : (s + 1) * size], back_im[s * size : (s + 1) * size]
        terms.append((re * tc - im * ts, im * tc + re * ts))
    for a in range(times):
        re, im = weighted(terms, [a * s for s in range(times)])
        back[a, :nb] = re.reshape(nb, rows, time)
        back[a, nb:] = im.reshape(nb, rows, time)
    for j in range(times):
        outs[j][...] = back[z ^ j].astype(outs[j].dtype)


def part_kernel(times, *refs):
    blocks, (own, other), (held,) = refs[:times], refs[times : times + 2], refs[times + 2 :]
    core = lax.axis_index("pix") % 2
    z = lax.axis_index("tm")
    cut = blocks[0].shape[1] // 2
    for j in range(times):
        held[...] = blocks[j][...].astype(F32)
        at = pl.multiple_of((z ^ j) * cut, cut)
        mine = pl.multiple_of(core * cut, cut)
        theirs = pl.multiple_of((1 - core) * cut, cut)
        own[:, pl.ds(at, cut), :] = held[:, pl.ds(mine, cut), :]
        other[:, pl.ds(at, cut), :] = held[:, pl.ds(theirs, cut), :]


def join_kernel(starts, sizes, *refs):
    out = refs[-1]
    half = out.shape[1] // 2
    core = lax.axis_index("pix") % 2
    for n, (start, nb) in enumerate(zip(starts, sizes)):
        own, other = refs[2 * n], refs[2 * n + 1]
        for c in range(2):
            for b in range(nb):
                out[:, core * half + start + b, c, :] = own[c * nb + b]
                out[:, (1 - core) * half + start + b, c, :] = other[c * nb + b].astype(F32)


def tables(times, time):
    index = np.arange(time)
    angle = 2.0 * np.pi / time * (index[:, None] * index[None, :] % time)
    length = times * time
    twist = 2.0 * np.pi / length * (np.arange(times)[:, None] * index[None, :] % length)
    out = []
    for table in (np.cos(angle), np.sin(angle)):
        high = table.astype(np.float32).astype(jnp.bfloat16)
        low = (table - high.astype(np.float64)).astype(np.float32).astype(jnp.bfloat16)
        out += [jnp.asarray(high), jnp.asarray(low)]
    return out + [jnp.asarray(f(twist).astype(np.float32)) for f in (np.cos, np.sin)]


def fast_body(pix, times, fields, profiles, phase):
    modes, batch, _, time = fields.shape
    chips, half = pix // 2, batch // 2
    pixels = profiles.shape[0]
    rows = 2 * modes
    cut = rows // times
    scale = 1.0 / math.sqrt(pixels * pix)
    sizes = [half * part // sum(CHUNKS) for part in CHUNKS]
    starts = [sum(sizes[:n]) for n in range(len(sizes))]
    core = lax.axis_index("pix") % 2

    halves = call(
        functools.partial(split_kernel, starts, sizes),
        "split",
        [((2 * nb, modes, time), F32) for nb in sizes for _ in range(2)],
    )(fields)
    others = [swap_pix(halves[2 * n + 1], 1, pix) for n in range(len(sizes))]
    profiles_other = swap_pix(profiles, 1, pix)
    phase_other = swap_pix(phase, 1, pix)

    fulls, gathers = [], []
    for n, nb in enumerate(sizes):
        full, modal = call(
            modal_kernel, "modal", [((2 * nb, rows, time), F32), ((2 * nb, rows, time), BF16)]
        )(halves[2 * n], others[n])
        fulls.append(full)
        gathers.append([modal] + [swap_pix(modal, 2 * j, pix) for j in range(1, chips)])

    turn = call(
        functools.partial(turn_kernel, rows, chips), "turn", [((chips * rows, pixels), BF16)]
    )
    turned = turn(profiles)[0], turn(profiles_other)[0]

    low = jnp.where(core == 0, phase, phase_other)
    high = jnp.where(core == 0, phase_other, phase)
    angles = jnp.concatenate([low, high], axis=0).reshape(cut, time, times).transpose(2, 0, 1)
    phase_cos, phase_sin = jnp.cos(angles), jnp.sin(angles)
    consts = tables(times, time)

    finals = []
    for n, nb in enumerate(sizes):
        block = (2 * nb, rows, time)
        parts = call(
            functools.partial(kerr_kernel, nb, chips, 512),
            "kerr",
            [(block, F32)] + [(block, BF16)] * (chips - 1),
            [((chips * rows, 2 * time), BF16), ((2 * pixels, 2 * time), BF16)],
        )(profiles, profiles_other, *turned, *gathers[n])
        sums = [parts[0]] + [swap_pix(parts[j], 2 * j, pix) for j in range(1, chips)]
        block = (2 * nb, cut, time)
        pieces = call(
            functools.partial(step_kernel, nb, scale, times),
            "step",
            [(block, F32)] + [(block, BF16)] * (times - 1),
            [((2 * nb, rows, time), F32)],
        )(fulls[n], *sums)
        pieces = [pieces[0]] + [swap_tm(pieces[j], j, times) for j in range(1, times)]
        pieces = call(
            functools.partial(wave_kernel, nb, times),
            "wave",
            [(block, F32)] + [(block, BF16)] * (times - 1),
            [((times,) + block, F32)] * 2,
        )(*pieces, phase_cos, phase_sin, *consts)
        pieces = [pieces[0]] + [swap_tm(pieces[j], j, times) for j in range(1, times)]
        own, other = call(
            functools.partial(part_kernel, times),
            "part",
            [((2 * nb, modes, time), F32), ((2 * nb, modes, time), F32)],
            [(block, F32)],
        )(*pieces)
        finals += [own, swap_pix(other, 1, pix)]
    return call(functools.partial(join_kernel, starts, sizes), "join", [(fields.shape, F32)])(
        *finals
    )[0]


def split_length(length):
    first = 2 ** ((length.bit_length() - 1) // 2)
    return (first, length // first)


def small_table(size):
    index = jnp.arange(size, dtype=jnp.int32)
    product = index[:, None] * index[None, :] % size
    angles = product.astype(jnp.float32) * (2.0 * math.pi / size)
    return (jnp.cos(angles), jnp.sin(angles))


def twiddles(first, second, length):
    rows = jnp.arange(first, dtype=jnp.int32)
    cols = jnp.arange(second, dtype=jnp.int32)
    product = rows[:, None] * cols[None, :] % length
    angles = product.astype(jnp.float32) * (2.0 * math.pi / length)
    return (jnp.cos(angles), jnp.sin(angles))


def contract_last(values, table):
    return jnp.einsum(
        "mbkv,vq->mbkq",
        values,
        table,
        precision=lax.Precision.HIGHEST,
        preferred_element_type=jnp.float32,
    )


def contract_third(values, table):
    return jnp.einsum(
        "mbuv,uk->mbkv",
        values,
        table,
        precision=lax.Precision.HIGHEST,
        preferred_element_type=jnp.float32,
    )


def dispersed(values, phase_rows, length):
    first, second = split_length(length)
    cos_first, sin_first = small_table(first)
    cos_second, sin_second = small_table(second)
    twist_cos, twist_sin = twiddles(first, second, length)
    modes_here = values.shape[0]
    batch = values.shape[1]
    real_part = values[:, :, 0].reshape(modes_here, batch, first, second)
    imag_part = values[:, :, 1].reshape(modes_here, batch, first, second)
    section_re = contract_third(real_part, cos_first) + contract_third(imag_part, sin_first)
    section_im = contract_third(imag_part, cos_first) - contract_third(real_part, sin_first)
    turned_re = section_re * twist_cos + section_im * twist_sin
    turned_im = section_im * twist_cos - section_re * twist_sin
    freq_re = contract_last(turned_re, cos_second) + contract_last(turned_im, sin_second)
    freq_im = contract_last(turned_im, cos_second) - contract_last(turned_re, sin_second)
    ordered = jnp.transpose(phase_rows.reshape(modes_here, second, first), (0, 2, 1))[:, None]
    phase_cos = jnp.cos(ordered)
    phase_sin = jnp.sin(ordered)
    spun_re = freq_re * phase_cos - freq_im * phase_sin
    spun_im = freq_re * phase_sin + freq_im * phase_cos
    back_re = contract_last(spun_re, cos_second) - contract_last(spun_im, sin_second)
    back_im = contract_last(spun_im, cos_second) + contract_last(spun_re, sin_second)
    again_re = back_re * twist_cos - back_im * twist_sin
    again_im = back_im * twist_cos + back_re * twist_sin
    out_re = contract_third(again_re, cos_first) - contract_third(again_im, sin_first)
    out_im = contract_third(again_im, cos_first) + contract_third(again_re, sin_first)
    out_re = out_re.reshape(modes_here, batch, length) / length
    out_im = out_im.reshape(modes_here, batch, length) / length
    return jnp.stack([out_re, out_im], axis=2)


def body(fields, profiles, phase):
    mode_local = fields.shape[0]
    batch = fields.shape[1]
    time_local = fields.shape[3]
    pixel_local = profiles.shape[0]
    length = time_local * lax.axis_size("tm")
    scale = 1.0 / math.sqrt(pixel_local * lax.axis_size("pix"))
    modal = fields.astype(jnp.bfloat16)
    piece = lax.all_gather(modal, "pix", axis=0, tiled=True)
    columns = profiles
    spatial = jnp.dot(
        columns, piece.reshape(piece.shape[0], -1), preferred_element_type=jnp.float32
    )
    spatial = spatial.reshape(pixel_local, batch, 2, time_local)
    real_part = spatial[:, :, 0]
    imag_part = spatial[:, :, 1]
    power = real_part * real_part + imag_part * imag_part
    nonlin = (
        jnp.stack([power * real_part, power * imag_part], axis=2)
        .astype(jnp.bfloat16)
        .reshape(pixel_local, -1)
    )
    columns = profiles
    kerr = lax.psum_scatter(
        lax.dot_general(
            columns, nonlin, (((0,), (0,)), ((), ())), preferred_element_type=jnp.float32
        ),
        "pix",
        scatter_dimension=0,
        tiled=True,
    )
    kerr = kerr.reshape(mode_local, batch, 2, time_local) * scale
    stepped = jnp.stack([fields[:, :, 0] - kerr[:, :, 1], fields[:, :, 1] + kerr[:, :, 0]], axis=2)
    result = dispersed(
        lax.all_to_all(stepped, "tm", split_axis=0, concat_axis=3, tiled=True), phase, length
    )
    return lax.all_to_all(result, "tm", split_axis=3, concat_axis=0, tiled=True)


def solution(mesh):
    pix, times = mesh.shape["pix"], mesh.shape["tm"]

    def run(fields, profiles, phase):
        modes, batch, _, time = fields.shape
        fits = (
            pix % 2 == 0
            and pix & (pix - 1) == 0
            and times == 4
            and modes % (8 * times) == 0
            and batch % 2 == 0
            and time % 256 == 0
            and profiles.shape[0] % 512 == 0
        )
        if fits:
            return fast_body(pix, times, fields, profiles, phase)
        return body(fields, profiles, phase)

    return jax.shard_map(
        run,
        mesh=mesh,
        in_specs=(P("pix", None, None, "tm"), P("pix", None), P(("pix", "tm"), None)),
        out_specs=P("pix", None, None, "tm"),
        check_vma=False,
    )
```

```python
import functools
import math

import jax
import jax.numpy as jnp
import numpy as np
from jax import lax
from jax.experimental import pallas as pl
from jax.experimental.pallas import tpu as pltpu
from jax.sharding import PartitionSpec as P

BF16 = jnp.bfloat16
F32 = jnp.float32
CHUNKS = (1, 1)
VMEM = pl.BlockSpec(memory_space=pltpu.VMEM)


def size_of(shape, dtype):
    return math.prod(shape) * jnp.dtype(dtype).itemsize


def call(kernel, name, outs, scratch=(), flops=0):
    def run(*args):
        moved = sum(size_of(item.shape, item.dtype) for item in args)
        moved += sum(size_of(*out) for out in outs)
        held = sum(size_of(*item) for item in scratch)
        return pl.pallas_call(
            kernel,
            out_shape=tuple(jax.ShapeDtypeStruct(*out) for out in outs),
            in_specs=[VMEM] * len(args),
            out_specs=tuple(VMEM for _ in outs),
            scratch_shapes=[pltpu.VMEM(*item) for item in scratch],
            compiler_params=pltpu.CompilerParams(vmem_limit_bytes=moved + held + 3 * 2**20),
            cost_estimate=pl.CostEstimate(flops=flops, bytes_accessed=moved, transcendentals=0),
            name=name,
        )(*args)

    return run


def swap_pix(value, mask, size):
    return lax.ppermute(value, "pix", [(i, i ^ mask) for i in range(size)])


def swap_tm(value, mask, size):
    return lax.ppermute(value, "tm", [(i, i ^ mask) for i in range(size)])


def split_kernel(starts, sizes, fields, *outs):
    half = fields.shape[1] // 2
    core = lax.axis_index("pix") % 2
    for n, (start, nb) in enumerate(zip(starts, sizes)):
        own, other = outs[2 * n], outs[2 * n + 1]
        for c in range(2):
            for b in range(nb):
                own[c * nb + b] = fields[:, core * half + start + b, c, :]
                other[c * nb + b] = fields[:, (1 - core) * half + start + b, c, :]


def modal_kernel(own, other, full, modal):
    rows = own.shape[1]
    core = lax.axis_index("pix") % 2
    mine = pl.multiple_of(core * rows, rows)
    theirs = pl.multiple_of((1 - core) * rows, rows)
    for k in range(own.shape[0]):
        value = own[k]
        full[k, pl.ds(mine, rows), :] = value
        modal[k, pl.ds(mine, rows), :] = value.astype(BF16)
        value = other[k]
        full[k, pl.ds(theirs, rows), :] = value
        modal[k, pl.ds(theirs, rows), :] = value.astype(BF16)


def turn_kernel(rows, chips, profiles, turned):
    chip = lax.axis_index("pix") // 2
    step = 256
    for i in range(profiles.shape[0] // step):
        block = profiles[i * step : (i + 1) * step, :].T
        for j in range(chips):
            place = pl.multiple_of((chip ^ j) * rows, rows)
            turned[pl.ds(place, rows), i * step : (i + 1) * step] = block[j * rows : (j + 1) * rows]


def kerr_kernel(nb, chips, tile, *refs):
    profiles, turned = refs[0:2], refs[2:4]
    blocks = refs[4 : 4 + chips]
    outs = refs[4 + chips : 4 + 2 * chips]
    gathered, cubed = refs[4 + 2 * chips :]
    chip = lax.axis_index("pix") // 2
    rows, time = blocks[0].shape[1:]
    pixels = profiles[0].shape[0]

    def one(b, carry):
        for j in range(chips):
            place = pl.multiple_of((chip ^ j) * rows, rows)
            for c in range(2):
                gathered[pl.ds(place, rows), c * time : (c + 1) * time] = blocks[j][c * nb + b]
        modal = gathered[...]
        for h in range(2):
            for i in range(pixels // tile):
                spatial = jnp.dot(
                    profiles[h][i * tile : (i + 1) * tile, :], modal, preferred_element_type=F32
                )
                real, imag = spatial[:, :time], spatial[:, time:]
                power = real * real + imag * imag
                at = h * pixels + i * tile
                cubed[at : at + tile, :time] = (power * real).astype(BF16)
                cubed[at : at + tile, time:] = (power * imag).astype(BF16)
        kerr = jnp.dot(turned[0][...], cubed[:pixels], preferred_element_type=F32) + jnp.dot(
            turned[1][...], cubed[pixels:], preferred_element_type=F32
        )
        for j in range(chips):
            for c in range(2):
                outs[j][c * nb + b] = kerr[
                    j * rows : (j + 1) * rows, c * time : (c + 1) * time
                ].astype(outs[j].dtype)
        return carry

    lax.fori_loop(0, nb, one, 0)


def step_kernel(nb, scale, times, full, *refs):
    chips = len(refs) - times - 1
    parts, outs, stepped = refs[:chips], refs[chips:-1], refs[-1]
    z = lax.axis_index("tm")
    rows = full.shape[1]
    cut = rows // 2 // times

    def total(k):
        value = parts[0][k]
        for part in parts[1:]:
            value = value + part[k].astype(F32)
        return value * scale

    for b in range(nb):
        stepped[b] = full[b] - total(nb + b)
        stepped[nb + b] = full[nb + b] + total(b)
    for j in range(times):
        for h in range(2):
            at = pl.multiple_of(h * (rows // 2) + (z ^ j) * cut, cut)
            for k in range(2 * nb):
                outs[j][k, h * cut : (h + 1) * cut, :] = stepped[k, pl.ds(at, cut), :].astype(
                    outs[j].dtype
                )


def product(value, high, low):
    top = value.astype(BF16)
    rest = (value - top.astype(F32)).astype(BF16)
    out = jnp.dot(top, high, preferred_element_type=F32)
    out = out + jnp.dot(rest, high, preferred_element_type=F32)
    return out + jnp.dot(top, low, preferred_element_type=F32)


def weighted(terms, powers):
    real, imag = None, None
    for (re, im), power in zip(terms, powers):
        re, im = ((re, im), (-im, re), (-re, -im), (im, -re))[power % 4]
        real = re if real is None else real + re
        imag = im if imag is None else imag + im
    return real, imag


def wave_kernel(sizes, times, *refs):
    count = len(sizes)
    blocks = refs[: times * count]
    phase_cos, phase_sin, cos_high, cos_low, sin_high, sin_low, twist_cos, twist_sin = refs[
        times * count : times * count + 8
    ]
    outs = refs[times * count + 8 : -2]
    held, back = refs[-2:]
    z = lax.axis_index("tm")
    nb = sum(sizes)
    rows, time = blocks[0].shape[1:]
    size = nb * rows
    length = times * time
    start = 0
    for n, part in enumerate(sizes):
        for j in range(times):
            block = blocks[n * times + j]
            for c in range(2):
                at = c * nb + start
                held[z ^ j, at : at + part] = block[c * part : (c + 1) * part].astype(F32)
        start += part
    here = [
        (held[a, :nb].reshape(size, time), held[a, nb:].reshape(size, time)) for a in range(times)
    ]
    real, imag = [], []
    for s in range(times):
        re, im = weighted(here, [-a * s for a in range(times)])
        tc, ts = twist_cos[s : s + 1, :], twist_sin[s : s + 1, :]
        real.append(re * tc + im * ts)
        imag.append(im * tc - re * ts)
    real, imag = jnp.concatenate(real, axis=0), jnp.concatenate(imag, axis=0)
    ch, cl, sh, sl = cos_high[...], cos_low[...], sin_high[...], sin_low[...]
    freq_re = product(real, ch, cl) + product(imag, sh, sl)
    freq_im = product(imag, ch, cl) - product(real, sh, sl)
    shape = (times, nb, rows, time)
    pc = jnp.broadcast_to(phase_cos[...][:, None], shape).reshape(times * size, time)
    ps = jnp.broadcast_to(phase_sin[...][:, None], shape).reshape(times * size, time)
    spun_re = freq_re * pc - freq_im * ps
    spun_im = freq_re * ps + freq_im * pc
    back_re = product(spun_re, ch, cl) - product(spun_im, sh, sl)
    back_im = product(spun_im, ch, cl) + product(spun_re, sh, sl)
    terms = []
    for s in range(times):
        tc, ts = twist_cos[s : s + 1, :] / length, twist_sin[s : s + 1, :] / length
        re, im = back_re[s * size : (s + 1) * size], back_im[s * size : (s + 1) * size]
        terms.append((re * tc - im * ts, im * tc + re * ts))
    for a in range(times):
        re, im = weighted(terms, [a * s for s in range(times)])
        back[a, :nb] = re.reshape(nb, rows, time)
        back[a, nb:] = im.reshape(nb, rows, time)
    for j in range(times):
        outs[j][...] = back[z ^ j].astype(outs[j].dtype)


def part_kernel(times, *refs):
    blocks, (own, other), (held, sent) = refs[:times], refs[times : times + 2], refs[times + 2 :]
    core = lax.axis_index("pix") % 2
    z = lax.axis_index("tm")
    cut = blocks[0].shape[1] // 2
    for j in range(times):
        held[...] = blocks[j][...].astype(F32)
        at = pl.multiple_of((z ^ j) * cut, cut)
        mine = pl.multiple_of(core * cut, cut)
        theirs = pl.multiple_of((1 - core) * cut, cut)
        own[:, pl.ds(at, cut), :] = held[:, pl.ds(mine, cut), :]
        sent[:, pl.ds(at, cut), :] = held[:, pl.ds(theirs, cut), :]
    other[...] = sent[...].astype(other.dtype)


def join_kernel(own, other, out):
    half = out.shape[1] // 2
    core = lax.axis_index("pix") % 2
    for c in range(2):
        for b in range(half):
            out[:, core * half + b, c, :] = own[c * half + b]
            out[:, (1 - core) * half + b, c, :] = other[c * half + b].astype(F32)


def tables(times, time):
    index = np.arange(time)
    angle = 2.0 * np.pi / time * (index[:, None] * index[None, :] % time)
    length = times * time
    twist = 2.0 * np.pi / length * (np.arange(times)[:, None] * index[None, :] % length)
    out = []
    for table in (np.cos(angle), np.sin(angle)):
        high = table.astype(np.float32).astype(jnp.bfloat16)
        low = (table - high.astype(np.float64)).astype(np.float32).astype(jnp.bfloat16)
        out += [jnp.asarray(high), jnp.asarray(low)]
    return out + [jnp.asarray(f(twist).astype(np.float32)) for f in (np.cos, np.sin)]


def fast_body(pix, times, fields, profiles, phase):
    modes, batch, _, time = fields.shape
    chips, half = pix // 2, batch // 2
    pixels = profiles.shape[0]
    rows = 2 * modes
    cut = rows // times
    scale = 1.0 / math.sqrt(pixels * pix)
    sizes = [half * part // sum(CHUNKS) for part in CHUNKS]
    starts = [sum(sizes[:n]) for n in range(len(sizes))]
    core = lax.axis_index("pix") % 2

    halves = call(
        functools.partial(split_kernel, starts, sizes),
        "split",
        [((2 * nb, modes, time), F32) for nb in sizes for _ in range(2)],
    )(fields)
    others = [swap_pix(halves[2 * n + 1], 1, pix) for n in range(len(sizes))]
    profiles_other = swap_pix(profiles, 1, pix)
    phase_other = swap_pix(phase, 1, pix)

    fulls, gathers = [], []
    for n, nb in enumerate(sizes):
        full, modal = call(
            modal_kernel, "modal", [((2 * nb, rows, time), F32), ((2 * nb, rows, time), BF16)]
        )(halves[2 * n], others[n])
        fulls.append(full)
        gathers.append([modal] + [swap_pix(modal, 2 * j, pix) for j in range(1, chips)])

    turn = call(
        functools.partial(turn_kernel, rows, chips), "turn", [((chips * rows, pixels), BF16)]
    )
    turned = turn(profiles)[0], turn(profiles_other)[0]

    low = jnp.where(core == 0, phase, phase_other)
    high = jnp.where(core == 0, phase_other, phase)
    angles = jnp.concatenate([low, high], axis=0).reshape(cut, time, times).transpose(2, 0, 1)
    phase_cos, phase_sin = jnp.cos(angles), jnp.sin(angles)
    consts = tables(times, time)

    waves = []
    for n, nb in enumerate(sizes):
        block = (2 * nb, rows, time)
        parts = call(
            functools.partial(kerr_kernel, nb, chips, 512),
            "kerr",
            [(block, F32)] + [(block, BF16)] * (chips - 1),
            [((chips * rows, 2 * time), BF16), ((2 * pixels, 2 * time), BF16)],
            flops=16 * pixels * chips * rows * nb * time,
        )(profiles, profiles_other, *turned, *gathers[n])
        sums = [parts[0]] + [swap_pix(parts[j], 2 * j, pix) for j in range(1, chips)]
        block = (2 * nb, cut, time)
        pieces = call(
            functools.partial(step_kernel, nb, scale, times),
            "step",
            [(block, F32)] + [(block, BF16)] * (times - 1),
            [((2 * nb, rows, time), F32)],
        )(fulls[n], *sums)
        waves += [pieces[0]] + [swap_tm(pieces[j], j, times) for j in range(1, times)]
    block = (2 * half, cut, time)
    pieces = call(
        functools.partial(wave_kernel, sizes, times),
        "wave",
        [(block, F32)] + [(block, BF16)] * (times - 1),
        [((times,) + block, F32)] * 2,
        flops=10**9,
    )(*waves, phase_cos, phase_sin, *consts)
    pieces = [pieces[0]] + [swap_tm(pieces[j], j, times) for j in range(1, times)]
    block = (2 * half, modes, time)
    own, other = call(
        functools.partial(part_kernel, times),
        "part",
        [(block, F32), (block, BF16)],
        [((2 * half, cut, time), F32), (block, F32)],
    )(*pieces)
    return call(join_kernel, "join", [(fields.shape, F32)])(own, swap_pix(other, 1, pix))[0]


def split_length(length):
    first = 2 ** ((length.bit_length() - 1) // 2)
    return (first, length // first)


def small_table(size):
    index = jnp.arange(size, dtype=jnp.int32)
    product = index[:, None] * index[None, :] % size
    angles = product.astype(jnp.float32) * (2.0 * math.pi / size)
    return (jnp.cos(angles), jnp.sin(angles))


def twiddles(first, second, length):
    rows = jnp.arange(first, dtype=jnp.int32)
    cols = jnp.arange(second, dtype=jnp.int32)
    product = rows[:, None] * cols[None, :] % length
    angles = product.astype(jnp.float32) * (2.0 * math.pi / length)
    return (jnp.cos(angles), jnp.sin(angles))


def contract_last(values, table):
    return jnp.einsum(
        "mbkv,vq->mbkq",
        values,
        table,
        precision=lax.Precision.HIGHEST,
        preferred_element_type=jnp.float32,
    )


def contract_third(values, table):
    return jnp.einsum(
        "mbuv,uk->mbkv",
        values,
        table,
        precision=lax.Precision.HIGHEST,
        preferred_element_type=jnp.float32,
    )


def dispersed(values, phase_rows, length):
    first, second = split_length(length)
    cos_first, sin_first = small_table(first)
    cos_second, sin_second = small_table(second)
    twist_cos, twist_sin = twiddles(first, second, length)
    modes_here = values.shape[0]
    batch = values.shape[1]
    real_part = values[:, :, 0].reshape(modes_here, batch, first, second)
    imag_part = values[:, :, 1].reshape(modes_here, batch, first, second)
    section_re = contract_third(real_part, cos_first) + contract_third(imag_part, sin_first)
    section_im = contract_third(imag_part, cos_first) - contract_third(real_part, sin_first)
    turned_re = section_re * twist_cos + section_im * twist_sin
    turned_im = section_im * twist_cos - section_re * twist_sin
    freq_re = contract_last(turned_re, cos_second) + contract_last(turned_im, sin_second)
    freq_im = contract_last(turned_im, cos_second) - contract_last(turned_re, sin_second)
    ordered = jnp.transpose(phase_rows.reshape(modes_here, second, first), (0, 2, 1))[:, None]
    phase_cos = jnp.cos(ordered)
    phase_sin = jnp.sin(ordered)
    spun_re = freq_re * phase_cos - freq_im * phase_sin
    spun_im = freq_re * phase_sin + freq_im * phase_cos
    back_re = contract_last(spun_re, cos_second) - contract_last(spun_im, sin_second)
    back_im = contract_last(spun_im, cos_second) + contract_last(spun_re, sin_second)
    again_re = back_re * twist_cos - back_im * twist_sin
    again_im = back_im * twist_cos + back_re * twist_sin
    out_re = contract_third(again_re, cos_first) - contract_third(again_im, sin_first)
    out_im = contract_third(again_im, cos_first) + contract_third(again_re, sin_first)
    out_re = out_re.reshape(modes_here, batch, length) / length
    out_im = out_im.reshape(modes_here, batch, length) / length
    return jnp.stack([out_re, out_im], axis=2)


def body(fields, profiles, phase):
    mode_local = fields.shape[0]
    batch = fields.shape[1]
    time_local = fields.shape[3]
    pixel_local = profiles.shape[0]
    length = time_local * lax.axis_size("tm")
    scale = 1.0 / math.sqrt(pixel_local * lax.axis_size("pix"))
    modal = fields.astype(jnp.bfloat16)
    piece = lax.all_gather(modal, "pix", axis=0, tiled=True)
    columns = profiles
    spatial = jnp.dot(
        columns, piece.reshape(piece.shape[0], -1), preferred_element_type=jnp.float32
    )
    spatial = spatial.reshape(pixel_local, batch, 2, time_local)
    real_part = spatial[:, :, 0]
    imag_part = spatial[:, :, 1]
    power = real_part * real_part + imag_part * imag_part
    nonlin = (
        jnp.stack([power * real_part, power * imag_part], axis=2)
        .astype(jnp.bfloat16)
        .reshape(pixel_local, -1)
    )
    columns = profiles
    kerr = lax.psum_scatter(
        lax.dot_general(
            columns, nonlin, (((0,), (0,)), ((), ())), preferred_element_type=jnp.float32
        ),
        "pix",
        scatter_dimension=0,
        tiled=True,
    )
    kerr = kerr.reshape(mode_local, batch, 2, time_local) * scale
    stepped = jnp.stack([fields[:, :, 0] - kerr[:, :, 1], fields[:, :, 1] + kerr[:, :, 0]], axis=2)
    result = dispersed(
        lax.all_to_all(stepped, "tm", split_axis=0, concat_axis=3, tiled=True), phase, length
    )
    return lax.all_to_all(result, "tm", split_axis=3, concat_axis=0, tiled=True)


def solution(mesh):
    pix, times = mesh.shape["pix"], mesh.shape["tm"]

    def run(fields, profiles, phase):
        modes, batch, _, time = fields.shape
        fits = (
            pix % 2 == 0
            and pix & (pix - 1) == 0
            and times == 4
            and modes % (8 * times) == 0
            and batch % 2 == 0
            and time % 256 == 0
            and profiles.shape[0] % 512 == 0
        )
        if fits:
            return fast_body(pix, times, fields, profiles, phase)
        return body(fields, profiles, phase)

    return jax.shard_map(
        run,
        mesh=mesh,
        in_specs=(P("pix", None, None, "tm"), P("pix", None), P(("pix", "tm"), None)),
        out_specs=P("pix", None, None, "tm"),
        check_vma=False,
    )
```

```python
import functools
import math

import jax
import jax.numpy as jnp
import numpy as np
from jax import lax
from jax.experimental import pallas as pl
from jax.experimental.pallas import tpu as pltpu
from jax.sharding import PartitionSpec as P


BF16 = jnp.bfloat16
F32 = jnp.float32
CHUNKS = (1, 1)
VMEM = pl.BlockSpec(memory_space=pltpu.VMEM)


def size_of(shape, dtype):
    return math.prod(shape) * jnp.dtype(dtype).itemsize


def call(kernel, outs, scratch=(), flops=0):
    def run(*args):
        moved = sum(size_of(item.shape, item.dtype) for item in args)
        moved += sum(size_of(*out) for out in outs)
        held = sum(size_of(*item) for item in scratch)
        return pl.pallas_call(
            kernel,
            out_shape=tuple(jax.ShapeDtypeStruct(*out) for out in outs),
            in_specs=[VMEM] * len(args),
            out_specs=tuple(VMEM for _ in outs),
            scratch_shapes=[pltpu.VMEM(*item) for item in scratch],
            compiler_params=pltpu.CompilerParams(vmem_limit_bytes=moved + held + 3 * 2**20),
            cost_estimate=pl.CostEstimate(flops=flops, bytes_accessed=moved, transcendentals=0),
        )(*args)

    return run


def swap_pix(value, mask, size):
    return lax.ppermute(value, "pix", [(i, i ^ mask) for i in range(size)])


def swap_tm(value, mask, size):
    return lax.ppermute(value, "tm", [(i, i ^ mask) for i in range(size)])


def split_kernel(starts, sizes, fields, *outs):
    half = fields.shape[1] // 2
    core = lax.axis_index("pix") % 2
    for n, (start, nb) in enumerate(zip(starts, sizes)):
        own, other = outs[2 * n], outs[2 * n + 1]
        for c in range(2):
            for b in range(nb):
                own[c * nb + b] = fields[:, core * half + start + b, c, :]
                other[c * nb + b] = fields[:, (1 - core) * half + start + b, c, :]


def modal_kernel(own, other, full, modal):
    rows = own.shape[1]
    core = lax.axis_index("pix") % 2
    mine = pl.multiple_of(core * rows, rows)
    theirs = pl.multiple_of((1 - core) * rows, rows)
    for k in range(own.shape[0]):
        value = own[k]
        full[k, pl.ds(mine, rows), :] = value
        modal[k, pl.ds(mine, rows), :] = value.astype(BF16)
        value = other[k]
        full[k, pl.ds(theirs, rows), :] = value
        modal[k, pl.ds(theirs, rows), :] = value.astype(BF16)


def turn_kernel(rows, chips, profiles, turned):
    chip = lax.axis_index("pix") // 2
    step = 256
    for i in range(profiles.shape[0] // step):
        block = profiles[i * step : (i + 1) * step, :].T
        for j in range(chips):
            place = pl.multiple_of((chip ^ j) * rows, rows)
            turned[pl.ds(place, rows), i * step : (i + 1) * step] = block[j * rows : (j + 1) * rows]


def kerr_kernel(nb, chips, tile, *refs):
    profiles, turned = refs[0:2], refs[2:4]
    blocks = refs[4 : 4 + chips]
    outs = refs[4 + chips : 4 + 2 * chips]
    gathered, cubed = refs[4 + 2 * chips :]
    chip = lax.axis_index("pix") // 2
    rows, time = blocks[0].shape[1:]
    pixels = profiles[0].shape[0]

    def one(b, carry):
        for j in range(chips):
            place = pl.multiple_of((chip ^ j) * rows, rows)
            for c in range(2):
                gathered[pl.ds(place, rows), c * time : (c + 1) * time] = blocks[j][c * nb + b]
        modal = gathered[...]
        for h in range(2):
            for i in range(pixels // tile):
                spatial = jnp.dot(
                    profiles[h][i * tile : (i + 1) * tile, :], modal, preferred_element_type=F32
                )
                real, imag = spatial[:, :time], spatial[:, time:]
                power = real * real + imag * imag
                at = h * pixels + i * tile
                cubed[at : at + tile, :time] = (power * real).astype(BF16)
                cubed[at : at + tile, time:] = (power * imag).astype(BF16)
        kerr = jnp.dot(turned[0][...], cubed[:pixels], preferred_element_type=F32) + jnp.dot(
            turned[1][...], cubed[pixels:], preferred_element_type=F32
        )
        for j in range(chips):
            for c in range(2):
                outs[j][c * nb + b] = kerr[
                    j * rows : (j + 1) * rows, c * time : (c + 1) * time
                ].astype(outs[j].dtype)
        return carry

    lax.fori_loop(0, nb, one, 0)


def step_kernel(nb, scale, times, earlier, full, *refs):
    carried, refs = refs[:earlier], refs[earlier:]
    chips = len(refs) - times - 1
    parts, outs, stepped = refs[:chips], refs[chips:-1], refs[-1]
    ahead = 0
    for block in carried:
        outs[1][ahead : ahead + block.shape[0]] = block[...]
        ahead += block.shape[0]
    z = lax.axis_index("tm")
    rows = full.shape[1]
    cut = rows // 2 // times

    def total(k):
        value = parts[0][k]
        for part in parts[1:]:
            value = value + part[k].astype(F32)
        return value * scale

    for b in range(nb):
        stepped[b] = full[b] - total(nb + b)
        stepped[nb + b] = full[nb + b] + total(b)
    for j in range(times):
        for h in range(2):
            at = pl.multiple_of(h * (rows // 2) + (z ^ j) * cut, cut)
            for k in range(2 * nb):
                to = k + (ahead if j == 1 else 0)
                outs[j][to, h * cut : (h + 1) * cut, :] = stepped[k, pl.ds(at, cut), :].astype(
                    outs[j].dtype
                )


def product(value, high, low):
    top = value.astype(BF16)
    rest = (value - top.astype(F32)).astype(BF16)
    out = jnp.dot(top, high, preferred_element_type=F32)
    out = out + jnp.dot(rest, high, preferred_element_type=F32)
    return out + jnp.dot(top, low, preferred_element_type=F32)


def weighted(terms, powers):
    real, imag = None, None
    for (re, im), power in zip(terms, powers):
        re, im = ((re, im), (-im, re), (-re, -im), (im, -re))[power % 4]
        real = re if real is None else real + re
        imag = im if imag is None else imag + im
    return real, imag


def wave_kernel(sizes, times, *refs):
    count = len(sizes)
    joint, refs = refs[0], refs[1:]
    each = times - 1
    blocks = refs[: each * count]
    phase_cos, phase_sin, cos_high, cos_low, sin_high, sin_low, twist_cos, twist_sin = refs[
        each * count : each * count + 8
    ]
    outs = refs[each * count + 8 : -2]
    held, back = refs[-2:]
    z = lax.axis_index("tm")
    nb = sum(sizes)
    rows, time = blocks[0].shape[1:]
    size = nb * rows
    length = times * time
    start = 0
    for n, part in enumerate(sizes):
        own, *far = blocks[n * each : (n + 1) * each]
        for j, block in enumerate([own, joint] + far):
            for c in range(2):
                at = c * nb + start
                take = c * part + (2 * start if j == 1 else 0)
                held[z ^ j, at : at + part] = block[take : take + part].astype(F32)
        start += part
    here = [
        (held[a, :nb].reshape(size, time), held[a, nb:].reshape(size, time)) for a in range(times)
    ]
    real, imag = [], []
    for s in range(times):
        re, im = weighted(here, [-a * s for a in range(times)])
        tc, ts = twist_cos[s : s + 1, :], twist_sin[s : s + 1, :]
        real.append(re * tc + im * ts)
        imag.append(im * tc - re * ts)
    real, imag = jnp.concatenate(real, axis=0), jnp.concatenate(imag, axis=0)
    ch, cl, sh, sl = cos_high[...], cos_low[...], sin_high[...], sin_low[...]
    freq_re = product(real, ch, cl) + product(imag, sh, sl)
    freq_im = product(imag, ch, cl) - product(real, sh, sl)
    shape = (times, nb, rows, time)
    pc = jnp.broadcast_to(phase_cos[...][:, None], shape).reshape(times * size, time)
    ps = jnp.broadcast_to(phase_sin[...][:, None], shape).reshape(times * size, time)
    spun_re = freq_re * pc - freq_im * ps
    spun_im = freq_re * ps + freq_im * pc
    back_re = product(spun_re, ch, cl) - product(spun_im, sh, sl)
    back_im = product(spun_im, ch, cl) + product(spun_re, sh, sl)
    terms = []
    for s in range(times):
        tc, ts = twist_cos[s : s + 1, :] / length, twist_sin[s : s + 1, :] / length
        re, im = back_re[s * size : (s + 1) * size], back_im[s * size : (s + 1) * size]
        terms.append((re * tc - im * ts, im * tc + re * ts))
    for a in range(times):
        re, im = weighted(terms, [a * s for s in range(times)])
        back[a, :nb] = re.reshape(nb, rows, time)
        back[a, nb:] = im.reshape(nb, rows, time)
    for j in range(times):
        outs[j][...] = back[z ^ j].astype(outs[j].dtype)


def part_kernel(times, *refs):
    blocks, (own, other), (held, sent) = refs[:times], refs[times : times + 2], refs[times + 2 :]
    core = lax.axis_index("pix") % 2
    z = lax.axis_index("tm")
    cut = blocks[0].shape[1] // 2
    for j in range(times):
        held[...] = blocks[j][...].astype(F32)
        at = pl.multiple_of((z ^ j) * cut, cut)
        mine = pl.multiple_of(core * cut, cut)
        theirs = pl.multiple_of((1 - core) * cut, cut)
        own[:, pl.ds(at, cut), :] = held[:, pl.ds(mine, cut), :]
        sent[:, pl.ds(at, cut), :] = held[:, pl.ds(theirs, cut), :]
    other[...] = sent[...].astype(other.dtype)


def join_kernel(own, other, out):
    half = out.shape[1] // 2
    core = lax.axis_index("pix") % 2
    for c in range(2):
        for b in range(half):
            out[:, core * half + b, c, :] = own[c * half + b]
            out[:, (1 - core) * half + b, c, :] = other[c * half + b].astype(F32)


def tables(times, time):
    index = np.arange(time)
    angle = 2.0 * np.pi / time * (index[:, None] * index[None, :] % time)
    length = times * time
    twist = 2.0 * np.pi / length * (np.arange(times)[:, None] * index[None, :] % length)
    out = []
    for table in (np.cos(angle), np.sin(angle)):
        high = table.astype(np.float32).astype(jnp.bfloat16)
        low = (table - high.astype(np.float64)).astype(np.float32).astype(jnp.bfloat16)
        out += [jnp.asarray(high), jnp.asarray(low)]
    return out + [jnp.asarray(f(twist).astype(np.float32)) for f in (np.cos, np.sin)]


def fast_body(pix, times, fields, profiles, phase):
    modes, batch, _, time = fields.shape
    chips, half = pix // 2, batch // 2
    pixels = profiles.shape[0]
    rows = 2 * modes
    cut = rows // times
    scale = 1.0 / math.sqrt(pixels * pix)
    sizes = [half * part // sum(CHUNKS) for part in CHUNKS]
    starts = [sum(sizes[:n]) for n in range(len(sizes))]
    core = lax.axis_index("pix") % 2

    halves = call(
        functools.partial(split_kernel, starts, sizes),
        [((2 * nb, modes, time), F32) for nb in sizes for _ in range(2)],
    )(fields)
    others = [swap_pix(halves[2 * n + 1], 1, pix) for n in range(len(sizes))]
    profiles_other = swap_pix(profiles, 1, pix)
    phase_other = swap_pix(phase, 1, pix)

    fulls, gathers = [], []
    for n, nb in enumerate(sizes):
        full, modal = call(
            modal_kernel, [((2 * nb, rows, time), F32), ((2 * nb, rows, time), BF16)]
        )(halves[2 * n], others[n])
        fulls.append(full)
        gathers.append([modal] + [swap_pix(modal, 2 * j, pix) for j in range(1, chips)])

    turn = call(functools.partial(turn_kernel, rows, chips), [((chips * rows, pixels), BF16)])
    turned = []
    for value in (profiles, profiles_other):
        turned += turn(value)

    low = jnp.where(core == 0, phase, phase_other)
    high = jnp.where(core == 0, phase_other, phase)
    angles = jnp.concatenate([low, high], axis=0).reshape(cut, time, times).transpose(2, 0, 1)
    phase_cos, phase_sin = jnp.cos(angles), jnp.sin(angles)
    consts = tables(times, time)

    waves, near = [], []
    for n, nb in enumerate(sizes):
        block = (2 * nb, rows, time)
        parts = call(
            functools.partial(kerr_kernel, nb, chips, 512),
            [(block, F32)] + [(block, BF16)] * (chips - 1),
            [((chips * rows, 2 * time), BF16), ((2 * pixels, 2 * time), BF16)],
            flops=16 * pixels * chips * rows * nb * time,
        )(profiles, profiles_other, *turned, *gathers[n])
        sums = [parts[0]] + [swap_pix(parts[j], 2 * j, pix) for j in range(1, chips)]
        block = (2 * nb, cut, time)
        last = n == len(sizes) - 1
        joint = (2 * half, cut, time) if last else block
        carried = near if last else []
        pieces = call(
            functools.partial(step_kernel, nb, scale, times, len(carried)),
            [(block, F32), (joint, BF16)] + [(block, BF16)] * (times - 2),
            [((2 * nb, rows, time), F32)],
        )(fulls[n], *carried, *sums)
        near.append(pieces[1])
        waves += [pieces[0]] + [swap_tm(pieces[j], j, times) for j in range(2, times)]
    waves = [swap_tm(near[-1], 1, times)] + waves
    block = (2 * half, cut, time)
    pieces = call(
        functools.partial(wave_kernel, sizes, times),
        [(block, F32)] + [(block, BF16)] * (times - 1),
        [((times,) + block, F32)] * 2,
        flops=10**9,
    )(*waves, phase_cos, phase_sin, *consts)
    pieces = [pieces[0]] + [swap_tm(pieces[j], j, times) for j in range(1, times)]
    block = (2 * half, modes, time)
    own, other = call(
        functools.partial(part_kernel, times),
        [(block, F32), (block, BF16)],
        [((2 * half, cut, time), F32), (block, F32)],
    )(*pieces)
    return call(join_kernel, [(fields.shape, F32)])(own, swap_pix(other, 1, pix))[0]


def split_length(length):
    first = 2 ** ((length.bit_length() - 1) // 2)
    return (first, length // first)


def small_table(size):
    index = jnp.arange(size, dtype=jnp.int32)
    product = index[:, None] * index[None, :] % size
    angles = product.astype(jnp.float32) * (2.0 * math.pi / size)
    return (jnp.cos(angles), jnp.sin(angles))


def twiddles(first, second, length):
    rows = jnp.arange(first, dtype=jnp.int32)
    cols = jnp.arange(second, dtype=jnp.int32)
    product = rows[:, None] * cols[None, :] % length
    angles = product.astype(jnp.float32) * (2.0 * math.pi / length)
    return (jnp.cos(angles), jnp.sin(angles))


def contract_last(values, table):
    return jnp.einsum(
        "mbkv,vq->mbkq",
        values,
        table,
        precision=lax.Precision.HIGHEST,
        preferred_element_type=jnp.float32,
    )


def contract_third(values, table):
    return jnp.einsum(
        "mbuv,uk->mbkv",
        values,
        table,
        precision=lax.Precision.HIGHEST,
        preferred_element_type=jnp.float32,
    )


def dispersed(values, phase_rows, length):
    first, second = split_length(length)
    cos_first, sin_first = small_table(first)
    cos_second, sin_second = small_table(second)
    twist_cos, twist_sin = twiddles(first, second, length)
    modes_here = values.shape[0]
    batch = values.shape[1]
    real_part = values[:, :, 0].reshape(modes_here, batch, first, second)
    imag_part = values[:, :, 1].reshape(modes_here, batch, first, second)
    section_re = contract_third(real_part, cos_first) + contract_third(imag_part, sin_first)
    section_im = contract_third(imag_part, cos_first) - contract_third(real_part, sin_first)
    turned_re = section_re * twist_cos + section_im * twist_sin
    turned_im = section_im * twist_cos - section_re * twist_sin
    freq_re = contract_last(turned_re, cos_second) + contract_last(turned_im, sin_second)
    freq_im = contract_last(turned_im, cos_second) - contract_last(turned_re, sin_second)
    ordered = jnp.transpose(phase_rows.reshape(modes_here, second, first), (0, 2, 1))[:, None]
    phase_cos = jnp.cos(ordered)
    phase_sin = jnp.sin(ordered)
    spun_re = freq_re * phase_cos - freq_im * phase_sin
    spun_im = freq_re * phase_sin + freq_im * phase_cos
    back_re = contract_last(spun_re, cos_second) - contract_last(spun_im, sin_second)
    back_im = contract_last(spun_im, cos_second) + contract_last(spun_re, sin_second)
    again_re = back_re * twist_cos - back_im * twist_sin
    again_im = back_im * twist_cos + back_re * twist_sin
    out_re = contract_third(again_re, cos_first) - contract_third(again_im, sin_first)
    out_im = contract_third(again_im, cos_first) + contract_third(again_re, sin_first)
    out_re = out_re.reshape(modes_here, batch, length) / length
    out_im = out_im.reshape(modes_here, batch, length) / length
    return jnp.stack([out_re, out_im], axis=2)


def body(fields, profiles, phase):
    mode_local = fields.shape[0]
    batch = fields.shape[1]
    time_local = fields.shape[3]
    pixel_local = profiles.shape[0]
    length = time_local * lax.axis_size("tm")
    scale = 1.0 / math.sqrt(pixel_local * lax.axis_size("pix"))
    modal = fields.astype(jnp.bfloat16)
    piece = lax.all_gather(modal, "pix", axis=0, tiled=True)
    columns = profiles
    spatial = jnp.dot(
        columns, piece.reshape(piece.shape[0], -1), preferred_element_type=jnp.float32
    )
    spatial = spatial.reshape(pixel_local, batch, 2, time_local)
    real_part = spatial[:, :, 0]
    imag_part = spatial[:, :, 1]
    power = real_part * real_part + imag_part * imag_part
    nonlin = (
        jnp.stack([power * real_part, power * imag_part], axis=2)
        .astype(jnp.bfloat16)
        .reshape(pixel_local, -1)
    )
    columns = profiles
    kerr = lax.psum_scatter(
        lax.dot_general(
            columns, nonlin, (((0,), (0,)), ((), ())), preferred_element_type=jnp.float32
        ),
        "pix",
        scatter_dimension=0,
        tiled=True,
    )
    kerr = kerr.reshape(mode_local, batch, 2, time_local) * scale
    stepped = jnp.stack([fields[:, :, 0] - kerr[:, :, 1], fields[:, :, 1] + kerr[:, :, 0]], axis=2)
    result = dispersed(
        lax.all_to_all(stepped, "tm", split_axis=0, concat_axis=3, tiled=True), phase, length
    )
    return lax.all_to_all(result, "tm", split_axis=3, concat_axis=0, tiled=True)


def solution(mesh):
    pix, times = mesh.shape["pix"], mesh.shape["tm"]

    def run(fields, profiles, phase):
        modes, batch, _, time = fields.shape
        fits = (
            pix % 2 == 0
            and pix & (pix - 1) == 0
            and times == 4
            and modes % (8 * times) == 0
            and batch % 2 == 0
            and time % 256 == 0
            and profiles.shape[0] % 512 == 0
        )
        if fits:
            return fast_body(pix, times, fields, profiles, phase)
        return body(fields, profiles, phase)

    return jax.shard_map(
        run,
        mesh=mesh,
        in_specs=(P("pix", None, None, "tm"), P("pix", None), P(("pix", "tm"), None)),
        out_specs=P("pix", None, None, "tm"),
        check_vma=False,
    )
```

```python
import functools
import math

import jax
import jax.numpy as jnp
import numpy as np
from jax import lax
from jax.experimental import pallas as pl
from jax.experimental.pallas import tpu as pltpu
from jax.sharding import PartitionSpec as P


BF16 = jnp.bfloat16
F32 = jnp.float32
CHUNKS = (1, 1)
VMEM = pl.BlockSpec(memory_space=pltpu.VMEM)


def size_of(shape, dtype):
    return math.prod(shape) * jnp.dtype(dtype).itemsize


def call(kernel, outs, scratch=(), flops=0):
    def run(*args):
        moved = sum(size_of(item.shape, item.dtype) for item in args)
        moved += sum(size_of(*out) for out in outs)
        held = sum(size_of(*item) for item in scratch)
        return pl.pallas_call(
            kernel,
            out_shape=tuple(jax.ShapeDtypeStruct(*out) for out in outs),
            in_specs=[VMEM] * len(args),
            out_specs=tuple(VMEM for _ in outs),
            scratch_shapes=[pltpu.VMEM(*item) for item in scratch],
            compiler_params=pltpu.CompilerParams(vmem_limit_bytes=moved + held + 3 * 2**20),
            cost_estimate=pl.CostEstimate(flops=flops, bytes_accessed=moved, transcendentals=0),
        )(*args)

    return run


def turned_mask(mask, core):
    if isinstance(core, int):
        return {1: 2, 2: 1}.get(mask, mask) if core else mask
    return mask ^ 3 * core if mask in (1, 2) else mask


def swap_pix(value, mask, size):
    return lax.ppermute(value, "pix", [(i, i ^ mask) for i in range(size)])


def swap_chip(value, mask, size):
    pairs = [(i, i ^ 2 * turned_mask(mask, i % 2)) for i in range(size)]
    return lax.ppermute(value, "pix", pairs)


def swap_tm(value, mask, size):
    return lax.ppermute(value, "tm", [(i, i ^ mask) for i in range(size)])


def split_kernel(starts, sizes, fields, *outs):
    half = fields.shape[1] // 2
    core = lax.axis_index("pix") % 2
    for n, (start, nb) in enumerate(zip(starts, sizes)):
        own, other = outs[2 * n], outs[2 * n + 1]
        for c in range(2):
            for b in range(nb):
                own[c * nb + b] = fields[:, core * half + start + b, c, :]
                other[c * nb + b] = fields[:, (1 - core) * half + start + b, c, :]


def modal_kernel(own, other, full, modal):
    rows = own.shape[1]
    core = lax.axis_index("pix") % 2
    mine = pl.multiple_of(core * rows, rows)
    theirs = pl.multiple_of((1 - core) * rows, rows)
    for k in range(own.shape[0]):
        value = own[k]
        full[k, pl.ds(mine, rows), :] = value
        modal[k, pl.ds(mine, rows), :] = value.astype(BF16)
        value = other[k]
        full[k, pl.ds(theirs, rows), :] = value
        modal[k, pl.ds(theirs, rows), :] = value.astype(BF16)


def turn_kernel(rows, chips, profiles, turned):
    chip, core = lax.axis_index("pix") // 2, lax.axis_index("pix") % 2
    step = 256
    for i in range(profiles.shape[0] // step):
        block = profiles[i * step : (i + 1) * step, :].T
        for j in range(chips):
            mask = chip ^ j
            mask = jnp.where((mask == 1) | (mask == 2), mask ^ 3 * core, mask)
            place = pl.multiple_of(mask * rows, rows)
            turned[pl.ds(place, rows), i * step : (i + 1) * step] = block[j * rows : (j + 1) * rows]


def kerr_kernel(nb, chips, tile, *refs):
    profiles, turned = refs[0:2], refs[2:4]
    blocks = refs[4 : 4 + chips]
    outs = refs[4 + chips : 4 + 2 * chips]
    gathered, cubed = refs[4 + 2 * chips :]
    chip, core = lax.axis_index("pix") // 2, lax.axis_index("pix") % 2
    rows, time = blocks[0].shape[1:]
    pixels = profiles[0].shape[0]

    def one(b, carry):
        for j in range(chips):
            place = pl.multiple_of((chip ^ turned_mask(j, core)) * rows, rows)
            for c in range(2):
                gathered[pl.ds(place, rows), c * time : (c + 1) * time] = blocks[j][c * nb + b]
        modal = gathered[...]
        for h in range(2):
            for i in range(pixels // tile):
                spatial = jnp.dot(
                    profiles[h][i * tile : (i + 1) * tile, :], modal, preferred_element_type=F32
                )
                real, imag = spatial[:, :time], spatial[:, time:]
                power = real * real + imag * imag
                at = h * pixels + i * tile
                cubed[at : at + tile, :time] = (power * real).astype(BF16)
                cubed[at : at + tile, time:] = (power * imag).astype(BF16)
        kerr = jnp.dot(turned[0][...], cubed[:pixels], preferred_element_type=F32) + jnp.dot(
            turned[1][...], cubed[pixels:], preferred_element_type=F32
        )
        for j in range(chips):
            for c in range(2):
                outs[j][c * nb + b] = kerr[
                    j * rows : (j + 1) * rows, c * time : (c + 1) * time
                ].astype(outs[j].dtype)
        return carry

    lax.fori_loop(0, nb, one, 0)


def step_kernel(nb, scale, times, earlier, full, *refs):
    carried, refs = refs[:earlier], refs[earlier:]
    chips = len(refs) - times - 1
    parts, outs, stepped = refs[:chips], refs[chips:-1], refs[-1]
    ahead = 0
    for block in carried:
        outs[1][ahead : ahead + block.shape[0]] = block[...]
        ahead += block.shape[0]
    z = lax.axis_index("tm")
    rows = full.shape[1]
    cut = rows // 2 // times

    def total(k):
        value = parts[0][k]
        for part in parts[1:]:
            value = value + part[k].astype(F32)
        return value * scale

    for b in range(nb):
        stepped[b] = full[b] - total(nb + b)
        stepped[nb + b] = full[nb + b] + total(b)
    for j in range(times):
        for h in range(2):
            at = pl.multiple_of(h * (rows // 2) + (z ^ j) * cut, cut)
            for k in range(2 * nb):
                to = k + (ahead if j == 1 else 0)
                outs[j][to, h * cut : (h + 1) * cut, :] = stepped[k, pl.ds(at, cut), :].astype(
                    outs[j].dtype
                )


def product(value, high, low):
    top = value.astype(BF16)
    rest = (value - top.astype(F32)).astype(BF16)
    out = jnp.dot(top, high, preferred_element_type=F32)
    out = out + jnp.dot(rest, high, preferred_element_type=F32)
    return out + jnp.dot(top, low, preferred_element_type=F32)


def weighted(terms, powers):
    real, imag = None, None
    for (re, im), power in zip(terms, powers):
        re, im = ((re, im), (-im, re), (-re, -im), (im, -re))[power % 4]
        real = re if real is None else real + re
        imag = im if imag is None else imag + im
    return real, imag


def wave_kernel(sizes, times, *refs):
    count = len(sizes)
    joint, refs = refs[0], refs[1:]
    each = times - 1
    blocks = refs[: each * count]
    phase_cos, phase_sin, cos_high, cos_low, sin_high, sin_low, twist_cos, twist_sin = refs[
        each * count : each * count + 8
    ]
    outs = refs[each * count + 8 : -2]
    held, back = refs[-2:]
    z = lax.axis_index("tm")
    nb = sum(sizes)
    rows, time = blocks[0].shape[1:]
    size = nb * rows
    length = times * time
    start = 0
    for n, part in enumerate(sizes):
        own, *far = blocks[n * each : (n + 1) * each]
        for j, block in enumerate([own, joint] + far):
            for c in range(2):
                at = c * nb + start
                take = c * part + (2 * start if j == 1 else 0)
                held[z ^ j, at : at + part] = block[take : take + part].astype(F32)
        start += part
    here = [
        (held[a, :nb].reshape(size, time), held[a, nb:].reshape(size, time)) for a in range(times)
    ]
    real, imag = [], []
    for s in range(times):
        re, im = weighted(here, [-a * s for a in range(times)])
        tc, ts = twist_cos[s : s + 1, :], twist_sin[s : s + 1, :]
        real.append(re * tc + im * ts)
        imag.append(im * tc - re * ts)
    real, imag = jnp.concatenate(real, axis=0), jnp.concatenate(imag, axis=0)
    ch, cl, sh, sl = cos_high[...], cos_low[...], sin_high[...], sin_low[...]
    freq_re = product(real, ch, cl) + product(imag, sh, sl)
    freq_im = product(imag, ch, cl) - product(real, sh, sl)
    shape = (times, nb, rows, time)
    pc = jnp.broadcast_to(phase_cos[...][:, None], shape).reshape(times * size, time)
    ps = jnp.broadcast_to(phase_sin[...][:, None], shape).reshape(times * size, time)
    spun_re = freq_re * pc - freq_im * ps
    spun_im = freq_re * ps + freq_im * pc
    back_re = product(spun_re, ch, cl) - product(spun_im, sh, sl)
    back_im = product(spun_im, ch, cl) + product(spun_re, sh, sl)
    terms = []
    for s in range(times):
        tc, ts = twist_cos[s : s + 1, :] / length, twist_sin[s : s + 1, :] / length
        re, im = back_re[s * size : (s + 1) * size], back_im[s * size : (s + 1) * size]
        terms.append((re * tc - im * ts, im * tc + re * ts))
    for a in range(times):
        re, im = weighted(terms, [a * s for s in range(times)])
        back[a, :nb] = re.reshape(nb, rows, time)
        back[a, nb:] = im.reshape(nb, rows, time)
    for j in range(times):
        outs[j][...] = back[z ^ j].astype(outs[j].dtype)


def part_kernel(times, *refs):
    blocks, (own, other), (held, sent) = refs[:times], refs[times : times + 2], refs[times + 2 :]
    core = lax.axis_index("pix") % 2
    z = lax.axis_index("tm")
    cut = blocks[0].shape[1] // 2
    for j in range(times):
        held[...] = blocks[j][...].astype(F32)
        at = pl.multiple_of((z ^ j) * cut, cut)
        mine = pl.multiple_of(core * cut, cut)
        theirs = pl.multiple_of((1 - core) * cut, cut)
        own[:, pl.ds(at, cut), :] = held[:, pl.ds(mine, cut), :]
        sent[:, pl.ds(at, cut), :] = held[:, pl.ds(theirs, cut), :]
    other[...] = sent[...].astype(other.dtype)


def join_kernel(own, other, out):
    half = out.shape[1] // 2
    core = lax.axis_index("pix") % 2
    for c in range(2):
        for b in range(half):
            out[:, core * half + b, c, :] = own[c * half + b]
            out[:, (1 - core) * half + b, c, :] = other[c * half + b].astype(F32)


def tables(times, time):
    index = np.arange(time)
    angle = 2.0 * np.pi / time * (index[:, None] * index[None, :] % time)
    length = times * time
    twist = 2.0 * np.pi / length * (np.arange(times)[:, None] * index[None, :] % length)
    out = []
    for table in (np.cos(angle), np.sin(angle)):
        high = table.astype(np.float32).astype(jnp.bfloat16)
        low = (table - high.astype(np.float64)).astype(np.float32).astype(jnp.bfloat16)
        out += [jnp.asarray(high), jnp.asarray(low)]
    return out + [jnp.asarray(f(twist).astype(np.float32)) for f in (np.cos, np.sin)]


def fast_body(pix, times, fields, profiles, phase):
    modes, batch, _, time = fields.shape
    chips, half = pix // 2, batch // 2
    pixels = profiles.shape[0]
    rows = 2 * modes
    cut = rows // times
    scale = 1.0 / math.sqrt(pixels * pix)
    sizes = [half * part // sum(CHUNKS) for part in CHUNKS]
    starts = [sum(sizes[:n]) for n in range(len(sizes))]
    core = lax.axis_index("pix") % 2

    halves = call(
        functools.partial(split_kernel, starts, sizes),
        [((2 * nb, modes, time), F32) for nb in sizes for _ in range(2)],
    )(fields)
    others = [swap_pix(halves[2 * n + 1], 1, pix) for n in range(len(sizes))]
    profiles_other = swap_pix(profiles, 1, pix)
    phase_other = swap_pix(phase, 1, pix)

    fulls, gathers = [], []
    for n, nb in enumerate(sizes):
        full, modal = call(
            modal_kernel, [((2 * nb, rows, time), F32), ((2 * nb, rows, time), BF16)]
        )(halves[2 * n], others[n])
        fulls.append(full)
        gathers.append([modal] + [swap_chip(modal, j, pix) for j in range(1, chips)])

    turn = call(functools.partial(turn_kernel, rows, chips), [((chips * rows, pixels), BF16)])
    turned = []
    for value in (profiles, profiles_other):
        turned += turn(value)

    low = jnp.where(core == 0, phase, phase_other)
    high = jnp.where(core == 0, phase_other, phase)
    angles = jnp.concatenate([low, high], axis=0).reshape(cut, time, times).transpose(2, 0, 1)
    phase_cos, phase_sin = jnp.cos(angles), jnp.sin(angles)
    consts = tables(times, time)

    waves, near = [], []
    for n, nb in enumerate(sizes):
        block = (2 * nb, rows, time)
        parts = call(
            functools.partial(kerr_kernel, nb, chips, 512),
            [(block, F32)] + [(block, BF16)] * (chips - 1),
            [((chips * rows, 2 * time), BF16), ((2 * pixels, 2 * time), BF16)],
            flops=16 * pixels * chips * rows * nb * time,
        )(profiles, profiles_other, *turned, *gathers[n])
        sums = [parts[0]] + [swap_chip(parts[j], j, pix) for j in range(1, chips)]
        block = (2 * nb, cut, time)
        last = n == len(sizes) - 1
        joint = (2 * half, cut, time) if last else block
        carried = near if last else []
        pieces = call(
            functools.partial(step_kernel, nb, scale, times, len(carried)),
            [(block, F32), (joint, BF16)] + [(block, BF16)] * (times - 2),
            [((2 * nb, rows, time), F32)],
        )(fulls[n], *carried, *sums)
        near.append(pieces[1])
        waves += [pieces[0]] + [swap_tm(pieces[j], j, times) for j in range(2, times)]
    waves = [swap_tm(near[-1], 1, times)] + waves
    block = (2 * half, cut, time)
    pieces = call(
        functools.partial(wave_kernel, sizes, times),
        [(block, F32)] + [(block, BF16)] * (times - 1),
        [((times,) + block, F32)] * 2,
        flops=10**9,
    )(*waves, phase_cos, phase_sin, *consts)
    pieces = [pieces[0]] + [swap_tm(pieces[j], j, times) for j in range(1, times)]
    block = (2 * half, modes, time)
    own, other = call(
        functools.partial(part_kernel, times),
        [(block, F32), (block, BF16)],
        [((2 * half, cut, time), F32), (block, F32)],
    )(*pieces)
    return call(join_kernel, [(fields.shape, F32)])(own, swap_pix(other, 1, pix))[0]


def split_length(length):
    first = 2 ** ((length.bit_length() - 1) // 2)
    return (first, length // first)


def small_table(size):
    index = jnp.arange(size, dtype=jnp.int32)
    product = index[:, None] * index[None, :] % size
    angles = product.astype(jnp.float32) * (2.0 * math.pi / size)
    return (jnp.cos(angles), jnp.sin(angles))


def twiddles(first, second, length):
    rows = jnp.arange(first, dtype=jnp.int32)
    cols = jnp.arange(second, dtype=jnp.int32)
    product = rows[:, None] * cols[None, :] % length
    angles = product.astype(jnp.float32) * (2.0 * math.pi / length)
    return (jnp.cos(angles), jnp.sin(angles))


def contract_last(values, table):
    return jnp.einsum(
        "mbkv,vq->mbkq",
        values,
        table,
        precision=lax.Precision.HIGHEST,
        preferred_element_type=jnp.float32,
    )


def contract_third(values, table):
    return jnp.einsum(
        "mbuv,uk->mbkv",
        values,
        table,
        precision=lax.Precision.HIGHEST,
        preferred_element_type=jnp.float32,
    )


def dispersed(values, phase_rows, length):
    first, second = split_length(length)
    cos_first, sin_first = small_table(first)
    cos_second, sin_second = small_table(second)
    twist_cos, twist_sin = twiddles(first, second, length)
    modes_here = values.shape[0]
    batch = values.shape[1]
    real_part = values[:, :, 0].reshape(modes_here, batch, first, second)
    imag_part = values[:, :, 1].reshape(modes_here, batch, first, second)
    section_re = contract_third(real_part, cos_first) + contract_third(imag_part, sin_first)
    section_im = contract_third(imag_part, cos_first) - contract_third(real_part, sin_first)
    turned_re = section_re * twist_cos + section_im * twist_sin
    turned_im = section_im * twist_cos - section_re * twist_sin
    freq_re = contract_last(turned_re, cos_second) + contract_last(turned_im, sin_second)
    freq_im = contract_last(turned_im, cos_second) - contract_last(turned_re, sin_second)
    ordered = jnp.transpose(phase_rows.reshape(modes_here, second, first), (0, 2, 1))[:, None]
    phase_cos = jnp.cos(ordered)
    phase_sin = jnp.sin(ordered)
    spun_re = freq_re * phase_cos - freq_im * phase_sin
    spun_im = freq_re * phase_sin + freq_im * phase_cos
    back_re = contract_last(spun_re, cos_second) - contract_last(spun_im, sin_second)
    back_im = contract_last(spun_im, cos_second) + contract_last(spun_re, sin_second)
    again_re = back_re * twist_cos - back_im * twist_sin
    again_im = back_im * twist_cos + back_re * twist_sin
    out_re = contract_third(again_re, cos_first) - contract_third(again_im, sin_first)
    out_im = contract_third(again_im, cos_first) + contract_third(again_re, sin_first)
    out_re = out_re.reshape(modes_here, batch, length) / length
    out_im = out_im.reshape(modes_here, batch, length) / length
    return jnp.stack([out_re, out_im], axis=2)


def body(fields, profiles, phase):
    mode_local = fields.shape[0]
    batch = fields.shape[1]
    time_local = fields.shape[3]
    pixel_local = profiles.shape[0]
    length = time_local * lax.axis_size("tm")
    scale = 1.0 / math.sqrt(pixel_local * lax.axis_size("pix"))
    modal = fields.astype(jnp.bfloat16)
    piece = lax.all_gather(modal, "pix", axis=0, tiled=True)
    columns = profiles
    spatial = jnp.dot(
        columns, piece.reshape(piece.shape[0], -1), preferred_element_type=jnp.float32
    )
    spatial = spatial.reshape(pixel_local, batch, 2, time_local)
    real_part = spatial[:, :, 0]
    imag_part = spatial[:, :, 1]
    power = real_part * real_part + imag_part * imag_part
    nonlin = (
        jnp.stack([power * real_part, power * imag_part], axis=2)
        .astype(jnp.bfloat16)
        .reshape(pixel_local, -1)
    )
    columns = profiles
    kerr = lax.psum_scatter(
        lax.dot_general(
            columns, nonlin, (((0,), (0,)), ((), ())), preferred_element_type=jnp.float32
        ),
        "pix",
        scatter_dimension=0,
        tiled=True,
    )
    kerr = kerr.reshape(mode_local, batch, 2, time_local) * scale
    stepped = jnp.stack([fields[:, :, 0] - kerr[:, :, 1], fields[:, :, 1] + kerr[:, :, 0]], axis=2)
    result = dispersed(
        lax.all_to_all(stepped, "tm", split_axis=0, concat_axis=3, tiled=True), phase, length
    )
    return lax.all_to_all(result, "tm", split_axis=3, concat_axis=0, tiled=True)


def solution(mesh):
    pix, times = mesh.shape["pix"], mesh.shape["tm"]

    def run(fields, profiles, phase):
        modes, batch, _, time = fields.shape
        fits = (
            pix % 2 == 0
            and pix & (pix - 1) == 0
            and times == 4
            and modes % (8 * times) == 0
            and batch % 2 == 0
            and time % 256 == 0
            and profiles.shape[0] % 512 == 0
        )
        if fits:
            return fast_body(pix, times, fields, profiles, phase)
        return body(fields, profiles, phase)

    return jax.shard_map(
        run,
        mesh=mesh,
        in_specs=(P("pix", None, None, "tm"), P("pix", None), P(("pix", "tm"), None)),
        out_specs=P("pix", None, None, "tm"),
        check_vma=False,
    )
```

```python
import functools
import math

import jax
import jax.numpy as jnp
import numpy as np
from jax import lax
from jax.experimental import pallas as pl
from jax.experimental.pallas import tpu as pltpu
from jax.sharding import PartitionSpec as P


BF16 = jnp.bfloat16
F32 = jnp.float32
CHUNKS = (1, 1)
VMEM = pl.BlockSpec(memory_space=pltpu.VMEM)


def size_of(shape, dtype):
    return math.prod(shape) * jnp.dtype(dtype).itemsize


def call(kernel, outs, scratch=(), flops=0):
    def run(*args):
        moved = sum(size_of(item.shape, item.dtype) for item in args)
        moved += sum(size_of(*out) for out in outs)
        held = sum(size_of(*item) for item in scratch)
        return pl.pallas_call(
            kernel,
            out_shape=tuple(jax.ShapeDtypeStruct(*out) for out in outs),
            in_specs=[VMEM] * len(args),
            out_specs=tuple(VMEM for _ in outs),
            scratch_shapes=[pltpu.VMEM(*item) for item in scratch],
            compiler_params=pltpu.CompilerParams(vmem_limit_bytes=moved + held + 3 * 2**20),
            cost_estimate=pl.CostEstimate(flops=flops, bytes_accessed=moved, transcendentals=0),
        )(*args)

    return run


def turned_mask(mask, core):
    if isinstance(core, int):
        return {1: 2, 2: 1}.get(mask, mask) if core else mask
    return mask ^ 3 * core if mask in (1, 2) else mask


def swap_pix(value, mask, size):
    return lax.ppermute(value, "pix", [(i, i ^ mask) for i in range(size)])


def swap_chip(value, mask, size):
    pairs = [(i, i ^ 2 * turned_mask(mask, i % 2)) for i in range(size)]
    return lax.ppermute(value, "pix", pairs)


def swap_tm(value, mask, size):
    return lax.ppermute(value, "tm", [(i, i ^ mask) for i in range(size)])


def split_kernel(starts, sizes, fields, *outs):
    half = fields.shape[1] // 2
    core = lax.axis_index("pix") % 2
    for n, (start, nb) in enumerate(zip(starts, sizes)):
        own, other = outs[2 * n], outs[2 * n + 1]
        for c in range(2):
            for b in range(nb):
                own[c * nb + b] = fields[:, core * half + start + b, c, :]
                other[c * nb + b] = fields[:, (1 - core) * half + start + b, c, :]


def modal_kernel(own, other, full, modal):
    rows = own.shape[1]
    core = lax.axis_index("pix") % 2
    mine = pl.multiple_of(core * rows, rows)
    theirs = pl.multiple_of((1 - core) * rows, rows)
    for k in range(own.shape[0]):
        value = own[k]
        full[k, pl.ds(mine, rows), :] = value
        modal[k, pl.ds(mine, rows), :] = value.astype(BF16)
        value = other[k]
        full[k, pl.ds(theirs, rows), :] = value
        modal[k, pl.ds(theirs, rows), :] = value.astype(BF16)


def turn_kernel(rows, chips, profiles, turned):
    chip, core = lax.axis_index("pix") // 2, lax.axis_index("pix") % 2
    step = 256
    for i in range(profiles.shape[0] // step):
        block = profiles[i * step : (i + 1) * step, :].T
        for j in range(chips):
            mask = chip ^ j
            mask = jnp.where((mask == 1) | (mask == 2), mask ^ 3 * core, mask)
            place = pl.multiple_of(mask * rows, rows)
            turned[pl.ds(place, rows), i * step : (i + 1) * step] = block[j * rows : (j + 1) * rows]


def kerr_kernel(nb, chips, tile, *refs):
    profiles, turned = refs[0:2], refs[2:4]
    blocks = refs[4 : 4 + chips]
    outs = refs[4 + chips : 4 + 2 * chips]
    gathered, cubed = refs[4 + 2 * chips :]
    chip, core = lax.axis_index("pix") // 2, lax.axis_index("pix") % 2
    rows, time = blocks[0].shape[1:]
    pixels = profiles[0].shape[0]

    def one(b, carry):
        for j in range(chips):
            place = pl.multiple_of((chip ^ turned_mask(j, core)) * rows, rows)
            for c in range(2):
                gathered[pl.ds(place, rows), c * time : (c + 1) * time] = blocks[j][c * nb + b]
        modal = gathered[...]
        for h in range(2):
            for i in range(pixels // tile):
                spatial = jnp.dot(
                    profiles[h][i * tile : (i + 1) * tile, :], modal, preferred_element_type=F32
                )
                real, imag = spatial[:, :time], spatial[:, time:]
                power = real * real + imag * imag
                at = h * pixels + i * tile
                cubed[at : at + tile, :time] = (power * real).astype(BF16)
                cubed[at : at + tile, time:] = (power * imag).astype(BF16)
        kerr = jnp.dot(turned[0][...], cubed[:pixels], preferred_element_type=F32) + jnp.dot(
            turned[1][...], cubed[pixels:], preferred_element_type=F32
        )
        for j in range(chips):
            for c in range(2):
                outs[j][c * nb + b] = kerr[
                    j * rows : (j + 1) * rows, c * time : (c + 1) * time
                ].astype(outs[j].dtype)
        return carry

    lax.fori_loop(0, nb, one, 0)


def step_kernel(nb, scale, times, earlier, full, *refs):
    carried, refs = refs[:earlier], refs[earlier:]
    chips = len(refs) - times - 1
    parts, outs, stepped = refs[:chips], refs[chips:-1], refs[-1]
    ahead = 0
    for block in carried:
        outs[1][ahead : ahead + block.shape[0]] = block[...]
        ahead += block.shape[0]
    z = lax.axis_index("tm")
    rows = full.shape[1]
    cut = rows // 2 // times

    def total(k):
        value = parts[0][k]
        for part in parts[1:]:
            value = value + part[k].astype(F32)
        return value * scale

    for b in range(nb):
        stepped[b] = full[b] - total(nb + b)
        stepped[nb + b] = full[nb + b] + total(b)
    for j in range(times):
        for h in range(2):
            at = pl.multiple_of(h * (rows // 2) + (z ^ j) * cut, cut)
            for k in range(2 * nb):
                to = k + (ahead if j == 1 else 0)
                outs[j][to, h * cut : (h + 1) * cut, :] = stepped[k, pl.ds(at, cut), :].astype(
                    outs[j].dtype
                )


def product(value, high, low):
    top = value.astype(BF16)
    rest = (value - top.astype(F32)).astype(BF16)
    out = jnp.dot(top, high, preferred_element_type=F32)
    out = out + jnp.dot(rest, high, preferred_element_type=F32)
    return out + jnp.dot(top, low, preferred_element_type=F32)


def weighted(terms, powers):
    real, imag = None, None
    for (re, im), power in zip(terms, powers):
        re, im = ((re, im), (-im, re), (-re, -im), (im, -re))[power % 4]
        real = re if real is None else real + re
        imag = im if imag is None else imag + im
    return real, imag


def wave_kernel(sizes, times, *refs):
    count = len(sizes)
    joint, refs = refs[0], refs[1:]
    each = times - 1
    blocks = refs[: each * count]
    phase_cos, phase_sin, cos_high, cos_low, sin_high, sin_low, twist_cos, twist_sin = refs[
        each * count : each * count + 8
    ]
    outs = refs[each * count + 8 : -2]
    held, back = refs[-2:]
    z = lax.axis_index("tm")
    nb = sum(sizes)
    rows, time = blocks[0].shape[1:]
    size = nb * rows
    length = times * time
    start = 0
    for n, part in enumerate(sizes):
        own, *far = blocks[n * each : (n + 1) * each]
        for j, block in enumerate([own, joint] + far):
            for c in range(2):
                at = c * nb + start
                take = c * part + (2 * start if j == 1 else 0)
                held[z ^ j, at : at + part] = block[take : take + part].astype(F32)
        start += part
    here = [
        (held[a, :nb].reshape(size, time), held[a, nb:].reshape(size, time)) for a in range(times)
    ]
    real, imag = [], []
    for s in range(times):
        re, im = weighted(here, [-a * s for a in range(times)])
        tc, ts = twist_cos[s : s + 1, :], twist_sin[s : s + 1, :]
        real.append(re * tc + im * ts)
        imag.append(im * tc - re * ts)
    real, imag = jnp.concatenate(real, axis=0), jnp.concatenate(imag, axis=0)
    ch, cl, sh, sl = cos_high[...], cos_low[...], sin_high[...], sin_low[...]
    freq_re = product(real, ch, cl) + product(imag, sh, sl)
    freq_im = product(imag, ch, cl) - product(real, sh, sl)
    shape = (times, nb, rows, time)
    pc = jnp.broadcast_to(phase_cos[...][:, None], shape).reshape(times * size, time)
    ps = jnp.broadcast_to(phase_sin[...][:, None], shape).reshape(times * size, time)
    spun_re = freq_re * pc - freq_im * ps
    spun_im = freq_re * ps + freq_im * pc
    back_re = product(spun_re, ch, cl) - product(spun_im, sh, sl)
    back_im = product(spun_im, ch, cl) + product(spun_re, sh, sl)
    terms = []
    for s in range(times):
        tc, ts = twist_cos[s : s + 1, :] / length, twist_sin[s : s + 1, :] / length
        re, im = back_re[s * size : (s + 1) * size], back_im[s * size : (s + 1) * size]
        terms.append((re * tc - im * ts, im * tc + re * ts))
    for a in range(times):
        re, im = weighted(terms, [a * s for s in range(times)])
        back[a, :nb] = re.reshape(nb, rows, time)
        back[a, nb:] = im.reshape(nb, rows, time)
    for j in range(times):
        outs[j][...] = back[z ^ j].astype(outs[j].dtype)


def part_kernel(times, *refs):
    blocks, (own, other), (held, sent) = refs[:times], refs[times : times + 2], refs[times + 2 :]
    core = lax.axis_index("pix") % 2
    z = lax.axis_index("tm")
    cut = blocks[0].shape[1] // 2
    for j in range(times):
        held[...] = blocks[j][...].astype(F32)
        at = pl.multiple_of((z ^ j) * cut, cut)
        mine = pl.multiple_of(core * cut, cut)
        theirs = pl.multiple_of((1 - core) * cut, cut)
        own[:, pl.ds(at, cut), :] = held[:, pl.ds(mine, cut), :]
        sent[:, pl.ds(at, cut), :] = held[:, pl.ds(theirs, cut), :]
    other[...] = sent[...].astype(other.dtype)


def join_kernel(mine, part, *refs):
    out, held, sem = refs[-3:]
    half = out.shape[1] // 2
    core = lax.axis_index("pix") % 2
    for c in range(2):
        for b in range(half):
            held[:, b, c, :] = part[c * half + b].astype(F32)
    which = core if mine else 1 - core
    copy = pltpu.make_async_copy(held, out.at[:, pl.ds(which * half, half)], sem)
    copy.start()
    copy.wait()


def join(part, shape, before=None):
    half = (shape[0], shape[1] // 2) + tuple(shape[2:])
    anywhere = pl.BlockSpec(memory_space=pl.ANY)
    args = (part,) if before is None else (part, before)
    moved = size_of(part.shape, part.dtype) + size_of(half, F32)
    return pl.pallas_call(
        functools.partial(join_kernel, before is None),
        out_shape=jax.ShapeDtypeStruct(shape, F32),
        in_specs=[VMEM] + [anywhere] * (len(args) - 1),
        out_specs=anywhere,
        scratch_shapes=[pltpu.VMEM(half, F32), pltpu.SemaphoreType.DMA],
        input_output_aliases={} if before is None else {1: 0},
        compiler_params=pltpu.CompilerParams(vmem_limit_bytes=2 * moved + 2**20),
        cost_estimate=pl.CostEstimate(flops=0, bytes_accessed=moved, transcendentals=0),
        name="join",
    )(*args)


def tables(times, time):
    index = np.arange(time)
    angle = 2.0 * np.pi / time * (index[:, None] * index[None, :] % time)
    length = times * time
    twist = 2.0 * np.pi / length * (np.arange(times)[:, None] * index[None, :] % length)
    out = []
    for table in (np.cos(angle), np.sin(angle)):
        high = table.astype(np.float32).astype(jnp.bfloat16)
        low = (table - high.astype(np.float64)).astype(np.float32).astype(jnp.bfloat16)
        out += [jnp.asarray(high), jnp.asarray(low)]
    return out + [jnp.asarray(f(twist).astype(np.float32)) for f in (np.cos, np.sin)]


def fast_body(pix, times, fields, profiles, phase):
    modes, batch, _, time = fields.shape
    chips, half = pix // 2, batch // 2
    pixels = profiles.shape[0]
    rows = 2 * modes
    cut = rows // times
    scale = 1.0 / math.sqrt(pixels * pix)
    sizes = [half * part // sum(CHUNKS) for part in CHUNKS]
    starts = [sum(sizes[:n]) for n in range(len(sizes))]
    core = lax.axis_index("pix") % 2

    halves = call(
        functools.partial(split_kernel, starts, sizes),
        [((2 * nb, modes, time), F32) for nb in sizes for _ in range(2)],
    )(fields)
    others = [swap_pix(halves[2 * n + 1], 1, pix) for n in range(len(sizes))]
    profiles_other = swap_pix(profiles, 1, pix)
    phase_other = swap_pix(phase, 1, pix)

    fulls, gathers = [], []
    for n, nb in enumerate(sizes):
        full, modal = call(
            modal_kernel, [((2 * nb, rows, time), F32), ((2 * nb, rows, time), BF16)]
        )(halves[2 * n], others[n])
        fulls.append(full)
        gathers.append([modal] + [swap_chip(modal, j, pix) for j in range(1, chips)])

    turn = call(functools.partial(turn_kernel, rows, chips), [((chips * rows, pixels), BF16)])
    turned = []
    for value in (profiles, profiles_other):
        turned += turn(value)

    low = jnp.where(core == 0, phase, phase_other)
    high = jnp.where(core == 0, phase_other, phase)
    angles = jnp.concatenate([low, high], axis=0).reshape(cut, time, times).transpose(2, 0, 1)
    phase_cos, phase_sin = jnp.cos(angles), jnp.sin(angles)
    consts = tables(times, time)

    waves, near = [], []
    for n, nb in enumerate(sizes):
        block = (2 * nb, rows, time)
        parts = call(
            functools.partial(kerr_kernel, nb, chips, 512),
            [(block, F32)] + [(block, BF16)] * (chips - 1),
            [((chips * rows, 2 * time), BF16), ((2 * pixels, 2 * time), BF16)],
            flops=16 * pixels * chips * rows * nb * time,
        )(profiles, profiles_other, *turned, *gathers[n])
        sums = [parts[0]] + [swap_chip(parts[j], j, pix) for j in range(1, chips)]
        block = (2 * nb, cut, time)
        last = n == len(sizes) - 1
        joint = (2 * half, cut, time) if last else block
        carried = near if last else []
        pieces = call(
            functools.partial(step_kernel, nb, scale, times, len(carried)),
            [(block, F32), (joint, BF16)] + [(block, BF16)] * (times - 2),
            [((2 * nb, rows, time), F32)],
        )(fulls[n], *carried, *sums)
        near.append(pieces[1])
        waves += [pieces[0]] + [swap_tm(pieces[j], j, times) for j in range(2, times)]
    waves = [swap_tm(near[-1], 1, times)] + waves
    block = (2 * half, cut, time)
    pieces = call(
        functools.partial(wave_kernel, sizes, times),
        [(block, F32)] + [(block, BF16)] * (times - 1),
        [((times,) + block, F32)] * 2,
        flops=10**9,
    )(*waves, phase_cos, phase_sin, *consts)
    pieces = [pieces[0]] + [swap_tm(pieces[j], j, times) for j in range(1, times)]
    block = (2 * half, modes, time)
    own, other = call(
        functools.partial(part_kernel, times),
        [(block, F32), (block, BF16)],
        [((2 * half, cut, time), F32), (block, F32)],
    )(*pieces)
    other = swap_pix(other, 1, pix)
    result = join(own, fields.shape)
    return join(other, fields.shape, result)


def split_length(length):
    first = 2 ** ((length.bit_length() - 1) // 2)
    return (first, length // first)


def small_table(size):
    index = jnp.arange(size, dtype=jnp.int32)
    product = index[:, None] * index[None, :] % size
    angles = product.astype(jnp.float32) * (2.0 * math.pi / size)
    return (jnp.cos(angles), jnp.sin(angles))


def twiddles(first, second, length):
    rows = jnp.arange(first, dtype=jnp.int32)
    cols = jnp.arange(second, dtype=jnp.int32)
    product = rows[:, None] * cols[None, :] % length
    angles = product.astype(jnp.float32) * (2.0 * math.pi / length)
    return (jnp.cos(angles), jnp.sin(angles))


def contract_last(values, table):
    return jnp.einsum(
        "mbkv,vq->mbkq",
        values,
        table,
        precision=lax.Precision.HIGHEST,
        preferred_element_type=jnp.float32,
    )


def contract_third(values, table):
    return jnp.einsum(
        "mbuv,uk->mbkv",
        values,
        table,
        precision=lax.Precision.HIGHEST,
        preferred_element_type=jnp.float32,
    )


def dispersed(values, phase_rows, length):
    first, second = split_length(length)
    cos_first, sin_first = small_table(first)
    cos_second, sin_second = small_table(second)
    twist_cos, twist_sin = twiddles(first, second, length)
    modes_here = values.shape[0]
    batch = values.shape[1]
    real_part = values[:, :, 0].reshape(modes_here, batch, first, second)
    imag_part = values[:, :, 1].reshape(modes_here, batch, first, second)
    section_re = contract_third(real_part, cos_first) + contract_third(imag_part, sin_first)
    section_im = contract_third(imag_part, cos_first) - contract_third(real_part, sin_first)
    turned_re = section_re * twist_cos + section_im * twist_sin
    turned_im = section_im * twist_cos - section_re * twist_sin
    freq_re = contract_last(turned_re, cos_second) + contract_last(turned_im, sin_second)
    freq_im = contract_last(turned_im, cos_second) - contract_last(turned_re, sin_second)
    ordered = jnp.transpose(phase_rows.reshape(modes_here, second, first), (0, 2, 1))[:, None]
    phase_cos = jnp.cos(ordered)
    phase_sin = jnp.sin(ordered)
    spun_re = freq_re * phase_cos - freq_im * phase_sin
    spun_im = freq_re * phase_sin + freq_im * phase_cos
    back_re = contract_last(spun_re, cos_second) - contract_last(spun_im, sin_second)
    back_im = contract_last(spun_im, cos_second) + contract_last(spun_re, sin_second)
    again_re = back_re * twist_cos - back_im * twist_sin
    again_im = back_im * twist_cos + back_re * twist_sin
    out_re = contract_third(again_re, cos_first) - contract_third(again_im, sin_first)
    out_im = contract_third(again_im, cos_first) + contract_third(again_re, sin_first)
    out_re = out_re.reshape(modes_here, batch, length) / length
    out_im = out_im.reshape(modes_here, batch, length) / length
    return jnp.stack([out_re, out_im], axis=2)


def body(fields, profiles, phase):
    mode_local = fields.shape[0]
    batch = fields.shape[1]
    time_local = fields.shape[3]
    pixel_local = profiles.shape[0]
    length = time_local * lax.axis_size("tm")
    scale = 1.0 / math.sqrt(pixel_local * lax.axis_size("pix"))
    modal = fields.astype(jnp.bfloat16)
    piece = lax.all_gather(modal, "pix", axis=0, tiled=True)
    columns = profiles
    spatial = jnp.dot(
        columns, piece.reshape(piece.shape[0], -1), preferred_element_type=jnp.float32
    )
    spatial = spatial.reshape(pixel_local, batch, 2, time_local)
    real_part = spatial[:, :, 0]
    imag_part = spatial[:, :, 1]
    power = real_part * real_part + imag_part * imag_part
    nonlin = (
        jnp.stack([power * real_part, power * imag_part], axis=2)
        .astype(jnp.bfloat16)
        .reshape(pixel_local, -1)
    )
    columns = profiles
    kerr = lax.psum_scatter(
        lax.dot_general(
            columns, nonlin, (((0,), (0,)), ((), ())), preferred_element_type=jnp.float32
        ),
        "pix",
        scatter_dimension=0,
        tiled=True,
    )
    kerr = kerr.reshape(mode_local, batch, 2, time_local) * scale
    stepped = jnp.stack([fields[:, :, 0] - kerr[:, :, 1], fields[:, :, 1] + kerr[:, :, 0]], axis=2)
    result = dispersed(
        lax.all_to_all(stepped, "tm", split_axis=0, concat_axis=3, tiled=True), phase, length
    )
    return lax.all_to_all(result, "tm", split_axis=3, concat_axis=0, tiled=True)


def solution(mesh):
    pix, times = mesh.shape["pix"], mesh.shape["tm"]

    def run(fields, profiles, phase):
        modes, batch, _, time = fields.shape
        fits = (
            pix % 2 == 0
            and pix & (pix - 1) == 0
            and times == 4
            and modes % (8 * times) == 0
            and batch % 2 == 0
            and time % 256 == 0
            and profiles.shape[0] % 512 == 0
        )
        if fits:
            return fast_body(pix, times, fields, profiles, phase)
        return body(fields, profiles, phase)

    return jax.shard_map(
        run,
        mesh=mesh,
        in_specs=(P("pix", None, None, "tm"), P("pix", None), P(("pix", "tm"), None)),
        out_specs=P("pix", None, None, "tm"),
        check_vma=False,
    )
```

```python
import functools
import math

import jax
import jax.numpy as jnp
import numpy as np
from jax import lax
from jax.experimental import pallas as pl
from jax.experimental.pallas import tpu as pltpu
from jax.sharding import PartitionSpec as P


BF16 = jnp.bfloat16
F32 = jnp.float32
CHUNKS = (1, 1)
VMEM = pl.BlockSpec(memory_space=pltpu.VMEM)


def size_of(shape, dtype):
    return math.prod(shape) * jnp.dtype(dtype).itemsize


def call(kernel, outs, scratch=(), flops=0):
    def run(*args):
        moved = sum(size_of(item.shape, item.dtype) for item in args)
        moved += sum(size_of(*out) for out in outs)
        held = sum(size_of(*item) for item in scratch)
        return pl.pallas_call(
            kernel,
            out_shape=tuple(jax.ShapeDtypeStruct(*out) for out in outs),
            in_specs=[VMEM] * len(args),
            out_specs=tuple(VMEM for _ in outs),
            scratch_shapes=[pltpu.VMEM(*item) for item in scratch],
            compiler_params=pltpu.CompilerParams(vmem_limit_bytes=moved + held + 3 * 2**20),
            cost_estimate=pl.CostEstimate(flops=flops, bytes_accessed=moved, transcendentals=0),
        )(*args)

    return run


def turned_mask(mask, core):
    if isinstance(core, int):
        return {1: 2, 2: 1}.get(mask, mask) if core else mask
    return mask ^ 3 * core if mask in (1, 2) else mask


def swap_pix(value, mask, size):
    return lax.ppermute(value, "pix", [(i, i ^ mask) for i in range(size)])


def swap_chip(value, mask, size):
    pairs = [(i, i ^ 2 * turned_mask(mask, i % 2)) for i in range(size)]
    return lax.ppermute(value, "pix", pairs)


def swap_tm(value, mask, size):
    return lax.ppermute(value, "tm", [(i, i ^ mask) for i in range(size)])


def split_kernel(starts, sizes, fields, *outs):
    half = fields.shape[1] // 2
    core = lax.axis_index("pix") % 2
    for n, (start, nb) in enumerate(zip(starts, sizes)):
        own, other = outs[2 * n], outs[2 * n + 1]
        for c in range(2):
            for b in range(nb):
                own[c * nb + b] = fields[:, core * half + start + b, c, :]
                other[c * nb + b] = fields[:, (1 - core) * half + start + b, c, :]


def modal_kernel(own, other, full, modal):
    rows = own.shape[1]
    core = lax.axis_index("pix") % 2
    mine = pl.multiple_of(core * rows, rows)
    theirs = pl.multiple_of((1 - core) * rows, rows)
    for k in range(own.shape[0]):
        value = own[k]
        full[k, pl.ds(mine, rows), :] = value
        modal[k, pl.ds(mine, rows), :] = value.astype(BF16)
        value = other[k]
        full[k, pl.ds(theirs, rows), :] = value
        modal[k, pl.ds(theirs, rows), :] = value.astype(BF16)


def turn_kernel(rows, chips, profiles, turned):
    chip, core = lax.axis_index("pix") // 2, lax.axis_index("pix") % 2
    step = 256
    for i in range(profiles.shape[0] // step):
        block = profiles[i * step : (i + 1) * step, :].T
        for j in range(chips):
            mask = chip ^ j
            mask = jnp.where((mask == 1) | (mask == 2), mask ^ 3 * core, mask)
            place = pl.multiple_of(mask * rows, rows)
            turned[pl.ds(place, rows), i * step : (i + 1) * step] = block[j * rows : (j + 1) * rows]


def kerr_kernel(nb, chips, tile, *refs):
    profiles, turned = refs[0:2], refs[2:4]
    blocks = refs[4 : 4 + chips]
    outs = refs[4 + chips : 4 + 2 * chips]
    gathered, cubed = refs[4 + 2 * chips :]
    chip, core = lax.axis_index("pix") // 2, lax.axis_index("pix") % 2
    rows, time = blocks[0].shape[1:]
    pixels = profiles[0].shape[0]

    def one(b, carry):
        for j in range(chips):
            place = pl.multiple_of((chip ^ turned_mask(j, core)) * rows, rows)
            for c in range(2):
                gathered[pl.ds(place, rows), c * time : (c + 1) * time] = blocks[j][c * nb + b]
        modal = gathered[...]
        for h in range(2):
            for i in range(pixels // tile):
                spatial = jnp.dot(
                    profiles[h][i * tile : (i + 1) * tile, :], modal, preferred_element_type=F32
                )
                real, imag = spatial[:, :time], spatial[:, time:]
                power = real * real + imag * imag
                at = h * pixels + i * tile
                cubed[at : at + tile, :time] = (power * real).astype(BF16)
                cubed[at : at + tile, time:] = (power * imag).astype(BF16)
        kerr = jnp.dot(turned[0][...], cubed[:pixels], preferred_element_type=F32) + jnp.dot(
            turned[1][...], cubed[pixels:], preferred_element_type=F32
        )
        for j in range(chips):
            for c in range(2):
                outs[j][c * nb + b] = kerr[
                    j * rows : (j + 1) * rows, c * time : (c + 1) * time
                ].astype(outs[j].dtype)
        return carry

    lax.fori_loop(0, nb, one, 0)


def step_kernel(nb, scale, times, earlier, full, *refs):
    carried, refs = refs[:earlier], refs[earlier:]
    chips = len(refs) - times - 1
    parts, outs, stepped = refs[:chips], refs[chips:-1], refs[-1]
    ahead = 0
    for block in carried:
        outs[1][ahead : ahead + block.shape[0]] = block[...]
        ahead += block.shape[0]
    z = lax.axis_index("tm")
    rows = full.shape[1]
    cut = rows // 2 // times

    def total(k):
        value = parts[0][k]
        for part in parts[1:]:
            value = value + part[k].astype(F32)
        return value * scale

    for b in range(nb):
        stepped[b] = full[b] - total(nb + b)
        stepped[nb + b] = full[nb + b] + total(b)
    for j in range(times):
        for h in range(2):
            at = pl.multiple_of(h * (rows // 2) + (z ^ j) * cut, cut)
            for k in range(2 * nb):
                to = k + (ahead if j == 1 else 0)
                outs[j][to, h * cut : (h + 1) * cut, :] = stepped[k, pl.ds(at, cut), :].astype(
                    outs[j].dtype
                )


def product(value, high, low):
    top = value.astype(BF16)
    rest = (value - top.astype(F32)).astype(BF16)
    out = jnp.dot(top, high, preferred_element_type=F32)
    out = out + jnp.dot(rest, high, preferred_element_type=F32)
    return out + jnp.dot(top, low, preferred_element_type=F32)


def weighted(terms, powers):
    real, imag = None, None
    for (re, im), power in zip(terms, powers):
        re, im = ((re, im), (-im, re), (-re, -im), (im, -re))[power % 4]
        real = re if real is None else real + re
        imag = im if imag is None else imag + im
    return real, imag


def wave_kernel(sizes, times, *refs):
    count = len(sizes)
    joint, refs = refs[0], refs[1:]
    each = times - 1
    blocks = refs[: each * count]
    phase_cos, phase_sin, cos_high, cos_low, less_high, less_low = refs[
        each * count : each * count + 6
    ]
    more_high, more_low, twist_cos, twist_sin = refs[each * count + 6 : each * count + 10]
    outs = refs[each * count + 10 : -2]
    held, back = refs[-2:]
    z = lax.axis_index("tm")
    nb = sum(sizes)
    rows, time = blocks[0].shape[1:]
    size = nb * rows
    length = times * time
    start = 0
    for n, part in enumerate(sizes):
        own, *far = blocks[n * each : (n + 1) * each]
        for j, block in enumerate([own, joint] + far):
            for c in range(2):
                at = c * nb + start
                take = c * part + (2 * start if j == 1 else 0)
                held[z ^ j, at : at + part] = block[take : take + part].astype(F32)
        start += part
    here = [
        (held[a, :nb].reshape(size, time), held[a, nb:].reshape(size, time)) for a in range(times)
    ]
    real, imag = [], []
    for s in range(times):
        re, im = weighted(here, [-a * s for a in range(times)])
        tc, ts = twist_cos[s : s + 1, :], twist_sin[s : s + 1, :]
        real.append(re * tc + im * ts)
        imag.append(im * tc - re * ts)
    real, imag = jnp.concatenate(real, axis=0), jnp.concatenate(imag, axis=0)
    ch, cl, dh, dl = cos_high[...], cos_low[...], less_high[...], less_low[...]
    eh, el = more_high[...], more_low[...]
    both = product(real + imag, ch, cl)
    freq_re = both - product(imag, dh, dl)
    freq_im = both - product(real, eh, el)
    shape = (times, nb, rows, time)
    pc = jnp.broadcast_to(phase_cos[...][:, None], shape).reshape(times * size, time)
    ps = jnp.broadcast_to(phase_sin[...][:, None], shape).reshape(times * size, time)
    spun_re = freq_re * pc - freq_im * ps
    spun_im = freq_re * ps + freq_im * pc
    both = product(spun_re + spun_im, ch, cl)
    back_re = both - product(spun_im, eh, el)
    back_im = both - product(spun_re, dh, dl)
    terms = []
    for s in range(times):
        tc, ts = twist_cos[s : s + 1, :] / length, twist_sin[s : s + 1, :] / length
        re, im = back_re[s * size : (s + 1) * size], back_im[s * size : (s + 1) * size]
        terms.append((re * tc - im * ts, im * tc + re * ts))
    for a in range(times):
        re, im = weighted(terms, [a * s for s in range(times)])
        back[a, :nb] = re.reshape(nb, rows, time)
        back[a, nb:] = im.reshape(nb, rows, time)
    for j in range(times):
        outs[j][...] = back[z ^ j].astype(outs[j].dtype)


def part_kernel(times, *refs):
    blocks, (own, other), (held, sent) = refs[:times], refs[times : times + 2], refs[times + 2 :]
    core = lax.axis_index("pix") % 2
    z = lax.axis_index("tm")
    cut = blocks[0].shape[1] // 2
    for j in range(times):
        held[...] = blocks[j][...].astype(F32)
        at = pl.multiple_of((z ^ j) * cut, cut)
        mine = pl.multiple_of(core * cut, cut)
        theirs = pl.multiple_of((1 - core) * cut, cut)
        own[:, pl.ds(at, cut), :] = held[:, pl.ds(mine, cut), :]
        sent[:, pl.ds(at, cut), :] = held[:, pl.ds(theirs, cut), :]
    other[...] = sent[...].astype(other.dtype)


def join_kernel(mine, part, *refs):
    out, held, sem = refs[-3:]
    half = out.shape[1] // 2
    core = lax.axis_index("pix") % 2
    for c in range(2):
        for b in range(half):
            held[:, b, c, :] = part[c * half + b].astype(F32)
    which = core if mine else 1 - core
    copy = pltpu.make_async_copy(held, out.at[:, pl.ds(which * half, half)], sem)
    copy.start()
    copy.wait()


def join(part, shape, before=None):
    half = (shape[0], shape[1] // 2) + tuple(shape[2:])
    anywhere = pl.BlockSpec(memory_space=pl.ANY)
    args = (part,) if before is None else (part, before)
    moved = size_of(part.shape, part.dtype) + size_of(half, F32)
    return pl.pallas_call(
        functools.partial(join_kernel, before is None),
        out_shape=jax.ShapeDtypeStruct(shape, F32),
        in_specs=[VMEM] + [anywhere] * (len(args) - 1),
        out_specs=anywhere,
        scratch_shapes=[pltpu.VMEM(half, F32), pltpu.SemaphoreType.DMA],
        input_output_aliases={} if before is None else {1: 0},
        compiler_params=pltpu.CompilerParams(vmem_limit_bytes=2 * moved + 2**20),
        cost_estimate=pl.CostEstimate(flops=0, bytes_accessed=moved, transcendentals=0),
        name="join",
    )(*args)


def tables(times, time):
    index = np.arange(time)
    angle = 2.0 * np.pi / time * (index[:, None] * index[None, :] % time)
    length = times * time
    twist = 2.0 * np.pi / length * (np.arange(times)[:, None] * index[None, :] % length)
    out = []
    cos, sin = np.cos(angle), np.sin(angle)
    for table in (cos, cos - sin, cos + sin):
        high = table.astype(np.float32).astype(jnp.bfloat16)
        low = (table - high.astype(np.float64)).astype(np.float32).astype(jnp.bfloat16)
        out += [jnp.asarray(high), jnp.asarray(low)]
    return out + [jnp.asarray(f(twist).astype(np.float32)) for f in (np.cos, np.sin)]


def fast_body(pix, times, fields, profiles, phase):
    modes, batch, _, time = fields.shape
    chips, half = pix // 2, batch // 2
    pixels = profiles.shape[0]
    rows = 2 * modes
    cut = rows // times
    scale = 1.0 / math.sqrt(pixels * pix)
    sizes = [half * part // sum(CHUNKS) for part in CHUNKS]
    starts = [sum(sizes[:n]) for n in range(len(sizes))]
    core = lax.axis_index("pix") % 2

    halves = call(
        functools.partial(split_kernel, starts, sizes),
        [((2 * nb, modes, time), F32) for nb in sizes for _ in range(2)],
    )(fields)
    others = [swap_pix(halves[2 * n + 1], 1, pix) for n in range(len(sizes))]
    profiles_other = swap_pix(profiles, 1, pix)
    phase_other = swap_pix(phase, 1, pix)

    fulls, gathers = [], []
    for n, nb in enumerate(sizes):
        full, modal = call(
            modal_kernel, [((2 * nb, rows, time), F32), ((2 * nb, rows, time), BF16)]
        )(halves[2 * n], others[n])
        fulls.append(full)
        gathers.append([modal] + [swap_chip(modal, j, pix) for j in range(1, chips)])

    turn = call(functools.partial(turn_kernel, rows, chips), [((chips * rows, pixels), BF16)])
    turned = []
    for value in (profiles, profiles_other):
        turned += turn(value)

    low = jnp.where(core == 0, phase, phase_other)
    high = jnp.where(core == 0, phase_other, phase)
    angles = jnp.concatenate([low, high], axis=0).reshape(cut, time, times).transpose(2, 0, 1)
    phase_cos, phase_sin = jnp.cos(angles), jnp.sin(angles)
    consts = tables(times, time)

    waves, near = [], []
    for n, nb in enumerate(sizes):
        block = (2 * nb, rows, time)
        parts = call(
            functools.partial(kerr_kernel, nb, chips, 512),
            [(block, F32)] + [(block, BF16)] * (chips - 1),
            [((chips * rows, 2 * time), BF16), ((2 * pixels, 2 * time), BF16)],
            flops=16 * pixels * chips * rows * nb * time,
        )(profiles, profiles_other, *turned, *gathers[n])
        sums = [parts[0]] + [swap_chip(parts[j], j, pix) for j in range(1, chips)]
        block = (2 * nb, cut, time)
        last = n == len(sizes) - 1
        joint = (2 * half, cut, time) if last else block
        carried = near if last else []
        pieces = call(
            functools.partial(step_kernel, nb, scale, times, len(carried)),
            [(block, F32), (joint, BF16)] + [(block, BF16)] * (times - 2),
            [((2 * nb, rows, time), F32)],
        )(fulls[n], *carried, *sums)
        near.append(pieces[1])
        waves += [pieces[0]] + [swap_tm(pieces[j], j, times) for j in range(2, times)]
    waves = [swap_tm(near[-1], 1, times)] + waves
    block = (2 * half, cut, time)
    pieces = call(
        functools.partial(wave_kernel, sizes, times),
        [(block, F32)] + [(block, BF16)] * (times - 1),
        [((times,) + block, F32)] * 2,
        flops=10**9,
    )(*waves, phase_cos, phase_sin, *consts)
    pieces = [pieces[0]] + [swap_tm(pieces[j], j, times) for j in range(1, times)]
    block = (2 * half, modes, time)
    own, other = call(
        functools.partial(part_kernel, times),
        [(block, F32), (block, BF16)],
        [((2 * half, cut, time), F32), (block, F32)],
    )(*pieces)
    other = swap_pix(other, 1, pix)
    result = join(own, fields.shape)
    return join(other, fields.shape, result)


def split_length(length):
    first = 2 ** ((length.bit_length() - 1) // 2)
    return (first, length // first)


def small_table(size):
    index = jnp.arange(size, dtype=jnp.int32)
    product = index[:, None] * index[None, :] % size
    angles = product.astype(jnp.float32) * (2.0 * math.pi / size)
    return (jnp.cos(angles), jnp.sin(angles))


def twiddles(first, second, length):
    rows = jnp.arange(first, dtype=jnp.int32)
    cols = jnp.arange(second, dtype=jnp.int32)
    product = rows[:, None] * cols[None, :] % length
    angles = product.astype(jnp.float32) * (2.0 * math.pi / length)
    return (jnp.cos(angles), jnp.sin(angles))


def contract_last(values, table):
    return jnp.einsum(
        "mbkv,vq->mbkq",
        values,
        table,
        precision=lax.Precision.HIGHEST,
        preferred_element_type=jnp.float32,
    )


def contract_third(values, table):
    return jnp.einsum(
        "mbuv,uk->mbkv",
        values,
        table,
        precision=lax.Precision.HIGHEST,
        preferred_element_type=jnp.float32,
    )


def dispersed(values, phase_rows, length):
    first, second = split_length(length)
    cos_first, sin_first = small_table(first)
    cos_second, sin_second = small_table(second)
    twist_cos, twist_sin = twiddles(first, second, length)
    modes_here = values.shape[0]
    batch = values.shape[1]
    real_part = values[:, :, 0].reshape(modes_here, batch, first, second)
    imag_part = values[:, :, 1].reshape(modes_here, batch, first, second)
    section_re = contract_third(real_part, cos_first) + contract_third(imag_part, sin_first)
    section_im = contract_third(imag_part, cos_first) - contract_third(real_part, sin_first)
    turned_re = section_re * twist_cos + section_im * twist_sin
    turned_im = section_im * twist_cos - section_re * twist_sin
    freq_re = contract_last(turned_re, cos_second) + contract_last(turned_im, sin_second)
    freq_im = contract_last(turned_im, cos_second) - contract_last(turned_re, sin_second)
    ordered = jnp.transpose(phase_rows.reshape(modes_here, second, first), (0, 2, 1))[:, None]
    phase_cos = jnp.cos(ordered)
    phase_sin = jnp.sin(ordered)
    spun_re = freq_re * phase_cos - freq_im * phase_sin
    spun_im = freq_re * phase_sin + freq_im * phase_cos
    back_re = contract_last(spun_re, cos_second) - contract_last(spun_im, sin_second)
    back_im = contract_last(spun_im, cos_second) + contract_last(spun_re, sin_second)
    again_re = back_re * twist_cos - back_im * twist_sin
    again_im = back_im * twist_cos + back_re * twist_sin
    out_re = contract_third(again_re, cos_first) - contract_third(again_im, sin_first)
    out_im = contract_third(again_im, cos_first) + contract_third(again_re, sin_first)
    out_re = out_re.reshape(modes_here, batch, length) / length
    out_im = out_im.reshape(modes_here, batch, length) / length
    return jnp.stack([out_re, out_im], axis=2)


def body(fields, profiles, phase):
    mode_local = fields.shape[0]
    batch = fields.shape[1]
    time_local = fields.shape[3]
    pixel_local = profiles.shape[0]
    length = time_local * lax.axis_size("tm")
    scale = 1.0 / math.sqrt(pixel_local * lax.axis_size("pix"))
    modal = fields.astype(jnp.bfloat16)
    piece = lax.all_gather(modal, "pix", axis=0, tiled=True)
    columns = profiles
    spatial = jnp.dot(
        columns, piece.reshape(piece.shape[0], -1), preferred_element_type=jnp.float32
    )
    spatial = spatial.reshape(pixel_local, batch, 2, time_local)
    real_part = spatial[:, :, 0]
    imag_part = spatial[:, :, 1]
    power = real_part * real_part + imag_part * imag_part
    nonlin = (
        jnp.stack([power * real_part, power * imag_part], axis=2)
        .astype(jnp.bfloat16)
        .reshape(pixel_local, -1)
    )
    columns = profiles
    kerr = lax.psum_scatter(
        lax.dot_general(
            columns, nonlin, (((0,), (0,)), ((), ())), preferred_element_type=jnp.float32
        ),
        "pix",
        scatter_dimension=0,
        tiled=True,
    )
    kerr = kerr.reshape(mode_local, batch, 2, time_local) * scale
    stepped = jnp.stack([fields[:, :, 0] - kerr[:, :, 1], fields[:, :, 1] + kerr[:, :, 0]], axis=2)
    result = dispersed(
        lax.all_to_all(stepped, "tm", split_axis=0, concat_axis=3, tiled=True), phase, length
    )
    return lax.all_to_all(result, "tm", split_axis=3, concat_axis=0, tiled=True)


def solution(mesh):
    pix, times = mesh.shape["pix"], mesh.shape["tm"]

    def run(fields, profiles, phase):
        modes, batch, _, time = fields.shape
        fits = (
            pix % 2 == 0
            and pix & (pix - 1) == 0
            and times == 4
            and modes % (8 * times) == 0
            and batch % 2 == 0
            and time % 256 == 0
            and profiles.shape[0] % 512 == 0
        )
        if fits:
            return fast_body(pix, times, fields, profiles, phase)
        return body(fields, profiles, phase)

    return jax.shard_map(
        run,
        mesh=mesh,
        in_specs=(P("pix", None, None, "tm"), P("pix", None), P(("pix", "tm"), None)),
        out_specs=P("pix", None, None, "tm"),
        check_vma=False,
    )
```
